256 devices in a mesh: slab: 16 (over x, z_lo, core), kern: 16 (over z_hi, y).
Axes of the slice: x: 4, y: 4, z: 8 (z_hi: 4, z_lo: 2; z = z_hi * 2 + z_lo), core: 2. Of those that a mesh axis runs over, the one named last changes fastest.
Arguments:
- mask_level: float32 [1024, 1024], P('slab'), may hold values from 0 to 1
- kernel_spectra: float32 [16, 2, 1024, 1024], P('kern', None, 'slab'), may hold values from -4.2 to 4.2
- socs_weight: float32 [16], replicated, may hold values from 0.05 to 0.5
- kernel_slot: int32 [16], replicated, may hold values from 0 to 15, each once
- blur_taps: float32 [31], replicated, may hold values from 0.005 to 0.06
- target: int32 [1024, 1024], P('slab'), may hold values 0 or 1
Outputs:
- mask_gradient: float32 [1024, 1024], P('slab', 'kern')
- resist_image: float32 [1024, 1024], P('slab', 'kern')
The draws below stay inside these ranges and needn't reach their ends.
Inputs may be any that keep to these rules, and one draw needn't show every extreme that they name: `target`: every cell is 0 or 1. `kernel_slot`: each kernel number stands at exactly one slot.
All inputs are finite; a program needn't handle non-finite values. No bound on the sum of `target` on one device may be relied on, other than what follows from the above.
Results may differ from the reference program's by a relative error of at most 0.00017.
Values sent between devices are 32-bit elements; how exact they have to be, the bound alone decides.
A program may use at most 64 MiB of HBM per device.

```python
import math
import jax
import jax.numpy as jnp
import numpy as np
from jax import lax

ROWS_DEV = 64
NG = 1024
KERNELS = 16
TAPS = 31
HALF = 15


def set_ends(entries, rng, smallest, largest):
    index_at = [jax.random.randint(jax.random.fold_in(rng, axis), (), 0, length) for axis, length in enumerate(entries.shape)]
    longest = entries.shape.index(max(entries.shape))
    next_to = index_at[:longest] + [(index_at[longest] + 1) % entries.shape[longest]] + index_at[longest + 1:]
    return entries.at[tuple(index_at)].set(smallest).at[tuple(next_to)].set(largest)


def levels(rng, shape, shards, least, top_value):
    def one(dim, shards_of):
        draws = jax.random.uniform(jax.random.fold_in(jax.random.fold_in(rng, 6), dim), (shards_of,), jnp.float32, least / len(shards), top_value / len(shards))
        return jnp.repeat(jnp.exp(draws), shape[dim] // shards_of).reshape((-1,) + (1,) * (len(shape) - dim - 1))

    factor_of = one(*shards[0])
    for cut in shards[1:]:
        factor_of = factor_of * one(*cut)
    return factor_of


def bell_draw(own_key, shape, scale, reach, shards=(), held_as=jnp.bfloat16):
    drawn = jax.random.normal(own_key, shape, jnp.float32) * scale
    if len(shards) > 0:
        drawn = levels(own_key, shape, shards, -0.22, 0.18) * drawn
    return jnp.clip(drawn, min=-reach, max=reach).astype(held_as)


def setup_inputs(seed: int = 0) -> dict:
    key_of = jax.random.split(jax.random.key(seed), 7)
    mask_level = jnp.clip(1.0 * jax.random.uniform(key_of[0], (NG, NG), jnp.float32) ** levels(key_of[0], (NG, NG), ((0, 16),), -0.2, 0.2), 0.0, 1.0)
    kernel_spectra = bell_draw(key_of[1], (KERNELS, 2, NG, NG), 0.7, 4.2, ((0, 16), (2, 16)), jnp.float32)
    socs_weight = jnp.clip(jnp.exp(jax.random.uniform(key_of[2], (KERNELS,), jnp.float32, math.log(0.05), math.log(0.5))), 0.05, 0.5)
    kernel_slot = jax.random.permutation(key_of[3], KERNELS).astype(jnp.int32)
    blur_taps = jnp.clip(jnp.exp(jax.random.uniform(key_of[4], (TAPS,), jnp.float32, math.log(0.005), math.log(0.06))), 0.005, 0.06)
    target = set_ends((jax.random.randint(key_of[5], (NG, NG), 0, 2) < 1).astype(jnp.int32), jax.random.fold_in(key_of[5], 1), 0, 1)
    return {"mask_level": mask_level, "kernel_spectra": kernel_spectra, "socs_weight": socs_weight, "kernel_slot": kernel_slot, "blur_taps": blur_taps, "target": target}


STEEP = 4.0
LEVEL = 0.5


def row_frequency():
    slab_count = NG // ROWS_DEV
    num_bits = slab_count.bit_length() - 1
    positions = np.arange(NG)
    device_idx = positions // ROWS_DEV
    flipped = device_idx * 0
    for bit_pos in range(num_bits):
        flipped = flipped * 2 + ((device_idx >> bit_pos) & 1)
    return flipped + slab_count * (positions % ROWS_DEV)


def smooth(values, kernel_taps):
    padded = jnp.pad(values, HALF)
    extent = values.shape[0]
    row_part = kernel_taps[0] * padded[0:extent, :]
    for tap_idx in range(1, TAPS):
        row_part = row_part + kernel_taps[tap_idx] * padded[tap_idx:tap_idx + extent, :]
    result = kernel_taps[0] * row_part[:, 0:extent]
    for tap_idx in range(1, TAPS):
        result = result + kernel_taps[tap_idx] * row_part[:, tap_idx:tap_idx + extent]
    return result


def reference(mask_level, kernel_spectra, socs_weight, kernel_slot, blur_taps, target):
    row_freq = row_frequency()
    inverse_order = np.argsort(row_freq)
    mask_spec = jnp.fft.fft2(mask_level)
    weights = socs_weight[kernel_slot]

    def kernel_field(kernel_idx):
        transfer = lax.complex(kernel_spectra[kernel_idx, 0], kernel_spectra[kernel_idx, 1])[inverse_order]
        return transfer, jnp.fft.ifft2(transfer * mask_spec)

    intensity = jnp.zeros((NG, NG), jnp.float32)
    for kernel_idx in range(KERNELS):
        transfer, field_val = kernel_field(kernel_idx)
        intensity = intensity + weights[kernel_idx] * (field_val.real ** 2 + field_val.imag ** 2)
    blurred = smooth(intensity, blur_taps)
    resist = jax.nn.sigmoid(STEEP * (blurred - LEVEL))
    slope_grad = 2.0 * (resist - target.astype(jnp.float32)) * STEEP * resist * (1.0 - resist)
    cotangent = smooth(slope_grad, blur_taps[::-1])
    gradient = jnp.zeros((NG, NG), jnp.float32)
    for kernel_idx in range(KERNELS):
        transfer, field_val = kernel_field(kernel_idx)
        factor = 2.0 * weights[kernel_idx] * cotangent
        carried = lax.complex(factor * field_val.real, factor * field_val.imag)
        gradient = gradient + jnp.fft.ifft2(jnp.conj(transfer) * jnp.fft.fft2(carried)).real
    return gradient, resist
```

```python
import math

import jax
import jax.numpy as jnp
from jax import lax
from jax.sharding import PartitionSpec as P

CQ = 128


STEEP = 4.0
LEVEL = 0.5


def swapped(shard, axis, apart):
    return lax.ppermute(shard, axis, [(i, i ^ 1 << apart) for i in range(lax.axis_size(axis))])


def padded_2(shard, sides, width):
    for axis, dim in sides:
        devices, length = (lax.axis_size(axis), shard.shape[dim])
        up = [(i, (i + 1) % devices) for i in range(devices - 1)]
        down = [(j, i) for i, j in up]
        last = lax.slice_in_dim(shard, length - width, length, axis=dim)
        initial = lax.slice_in_dim(shard, 0, width, axis=dim)
        before = lax.ppermute(last, axis, up)
        after = lax.ppermute(initial, axis, down)
        shard = jnp.concatenate([before, shard, after], axis=dim)
    return shard


def reversed_bits(number, num_bits):
    result = number * 0
    for bit_pos in range(num_bits):
        result = result * 2 + number // 2**bit_pos % 2
    return result


def rotation(product, length, sign_val):
    fraction = (product % length).astype(jnp.float32) / length
    angles = sign_val * 2.0 * math.pi * fraction
    return (jnp.cos(angles), jnp.sin(angles))


def complex_mul(first_pair, second_pair):
    real_part = first_pair[0] * second_pair[0] - first_pair[1] * second_pair[1]
    imag_part = first_pair[0] * second_pair[1] + first_pair[1] * second_pair[0]
    return (real_part, imag_part)


def table_product(pattern, matrix, values):
    highest = lax.Precision.HIGHEST

    def single(first_op, second_op):
        return jnp.einsum(pattern, first_op, second_op, precision=highest)

    if values[1] is None:
        return (single(matrix[0], values[0]), single(matrix[1], values[0]))
    real_part = single(matrix[0], values[0]) - single(matrix[1], values[1])
    imag_part = single(matrix[0], values[1]) + single(matrix[1], values[0])
    return (real_part, imag_part)


def columns_forward(values, outer_len, inner_len):
    extent = values[0].shape[0]
    shaped = tuple(
        (None if piece is None else piece.reshape(extent, outer_len, inner_len) for piece in values)
    )
    outer_idx = jnp.arange(outer_len)
    inner_idx = jnp.arange(inner_len)
    section = table_product(
        "ab,rbq->raq", rotation(outer_idx[:, None] * outer_idx[None, :], outer_len, -1.0), shaped
    )
    section = complex_mul(
        section, rotation(outer_idx[:, None] * inner_idx[None, :], outer_len * inner_len, -1.0)
    )
    return table_product(
        "bk,rpb->rpk", rotation(inner_idx[:, None] * inner_idx[None, :], inner_len, -1.0), section
    )


def columns_inverse(values, outer_len, inner_len, real_only):
    extent = values[0].shape[0]
    outer_idx = jnp.arange(outer_len)
    inner_idx = jnp.arange(inner_len)
    section = table_product(
        "bk,rpb->rpk", rotation(inner_idx[:, None] * inner_idx[None, :], inner_len, 1.0), values
    )
    section = complex_mul(
        section, rotation(outer_idx[:, None] * inner_idx[None, :], outer_len * inner_len, 1.0)
    )
    matrix = rotation(outer_idx[:, None] * outer_idx[None, :], outer_len, 1.0)
    if real_only:
        highest = lax.Precision.HIGHEST
        real_part = jnp.einsum("ab,rbq->raq", matrix[0], section[0], precision=highest)
        real_part = real_part - jnp.einsum("ab,rbq->raq", matrix[1], section[1], precision=highest)
        return real_part.reshape(extent, outer_len * inner_len)
    result = table_product("ab,rbq->raq", matrix, section)
    return (
        result[0].reshape(extent, outer_len * inner_len),
        result[1].reshape(extent, outer_len * inner_len),
    )


def rows_forward(values, freq_offset, full_width):
    extent = values[0].shape[0]
    positions = jnp.arange(extent)
    twiddle = rotation(positions * freq_offset, full_width, -1.0)
    values = complex_mul(values, (twiddle[0][:, None], twiddle[1][:, None]))
    return table_product(
        "sr,rc->sc", rotation(positions[:, None] * positions[None, :], extent, -1.0), values
    )


def rows_inverse(values, freq_offset, full_width):
    extent = values[0].shape[0]
    positions = jnp.arange(extent)
    values = table_product(
        "rs,sc->rc", rotation(positions[:, None] * positions[None, :], extent, 1.0), values
    )
    twiddle = rotation(positions * freq_offset, full_width, 1.0)
    return complex_mul(values, (twiddle[0][:, None], twiddle[1][:, None]))


def pairs_forward(stacked, num_bits):
    slab_index = lax.axis_index("slab")
    for bit_level in range(num_bits - 1, -1, -1):
        half_span = 2**bit_level
        partner = swapped(stacked, "slab", bit_level)
        is_upper = slab_index // half_span % 2 == 1
        twiddle = rotation(slab_index % half_span, 2 * half_span, -1.0)
        lower_val = stacked + partner
        difference = partner - stacked
        upper_val = jnp.stack(complex_mul((difference[0], difference[1]), twiddle))
        stacked = jnp.where(is_upper, upper_val, lower_val)
    return stacked


def pairs_inverse(stacked, num_bits):
    slab_index = lax.axis_index("slab")
    for bit_level in range(num_bits):
        half_span = 2**bit_level
        partner = swapped(stacked, "slab", bit_level)
        is_upper = slab_index // half_span % 2 == 1
        twiddle = rotation(slab_index % half_span, 2 * half_span, 1.0)
        from_upper = jnp.where(is_upper, stacked, partner)
        from_lower = jnp.where(is_upper, partner, stacked)
        turned = jnp.stack(complex_mul((from_upper[0], from_upper[1]), twiddle))
        stacked = jnp.where(is_upper, from_lower - turned, from_lower + turned)
    return stacked


def mix_forward(stacked, num_bits):
    return pairs_forward(stacked, num_bits)


def mix_inverse(stacked, num_bits):
    return pairs_inverse(stacked, num_bits)


def tap_band(kernel_taps, rows, cols, offset):
    diff = jnp.arange(rows)[:, None] - jnp.arange(cols)[None, :] - offset
    band = jnp.zeros((rows, cols), jnp.float32)
    for tap_idx in range(kernel_taps.shape[0]):
        band = band + jnp.where(diff == tap_idx, kernel_taps[tap_idx], 0.0)
    return band


def smooth(padded, kernel_taps, extent, span):
    highest = lax.Precision.HIGHEST
    reach = (kernel_taps.shape[0] - 1) // 2
    row_band = tap_band(kernel_taps, extent + 2 * reach, extent, 0).T
    row_part = jnp.dot(row_band, padded, precision=highest)
    block, margin = (128, 64)
    col_band = tap_band(kernel_taps, block + 2 * margin, block, margin - reach)
    widened = jnp.pad(row_part, ((0, 0), (margin, margin)))
    windows = jnp.stack(
        [widened[:, j * block : j * block + block + 2 * margin] for j in range(span // block)], 1
    )
    result = jnp.einsum("rji,ib->rjb", windows, col_band, precision=highest)
    return result.reshape(extent, span)


def reduce_scatter_cols(values, axis):
    count = lax.axis_size(axis)
    num_bits = count.bit_length() - 1
    index = lax.axis_index(axis)
    extent, width = values.shape
    values = values.reshape((extent,) + (2,) * num_bits + (width // count,))
    for bit_level in range(num_bits):
        dim = num_bits - bit_level
        mine = index // 2**bit_level % 2
        keep = lax.dynamic_index_in_dim(values, mine, axis=dim, keepdims=False)
        send = lax.dynamic_index_in_dim(values, 1 - mine, axis=dim, keepdims=False)
        values = keep + swapped(send, axis, bit_level)
    return values.reshape(extent, width // count)


def all_gather_cols(values, axis):
    count = lax.axis_size(axis)
    num_bits = count.bit_length() - 1
    index = lax.axis_index(axis)
    extent, block = values.shape
    for bit_level in range(num_bits - 1, -1, -1):
        got = swapped(values, axis, bit_level)
        is_upper = index // 2**bit_level % 2 == 1
        low = jnp.where(is_upper, got, values)
        high = jnp.where(is_upper, values, got)
        values = jnp.stack([low, high], values.ndim - 1)
    return values.reshape(extent, block * count)


def resist_section(intensity_term, kernel_taps, target, kern_count, kern_index):
    reach = (kernel_taps.shape[0] - 1) // 2
    flipped = kernel_taps[::-1]
    extent, full_width = intensity_term.shape
    share_cols = full_width // kern_count

    def widen(values):
        return padded_2(values, (("slab", 0),), reach)

    summed = all_gather_cols(reduce_scatter_cols(intensity_term, "kern"), "kern")
    goal_cells = target.astype(jnp.float32)
    resist = jax.nn.sigmoid(
        STEEP * (smooth(widen(summed), kernel_taps, extent, full_width) - LEVEL)
    )
    slope_grad = 2.0 * (resist - goal_cells) * STEEP * resist * (1.0 - resist)
    cotangent = smooth(widen(slope_grad), flipped, extent, full_width)
    return (cotangent, lax.dynamic_slice_in_dim(resist, kern_index * share_cols, share_cols, 1))


def on_device(mask_level, kernel_spectra, socs_weight, kernel_slot, blur_taps, target):
    extent, full_width = mask_level.shape
    slab_count = lax.axis_size("slab")
    kern_count = lax.axis_size("kern")
    num_bits = slab_count.bit_length() - 1
    inner_len = CQ
    outer_len = full_width // inner_len
    freq_offset = reversed_bits(lax.axis_index("slab"), num_bits)
    kern_index = lax.axis_index("kern")
    kernel_id = jnp.sum(jnp.where(jnp.arange(kernel_slot.shape[0]) == kern_index, kernel_slot, 0))
    weight = jnp.sum(jnp.where(jnp.arange(socs_weight.shape[0]) == kernel_id, socs_weight, 0.0))
    arranged = kernel_spectra[0].reshape(2, extent, inner_len, outer_len).transpose(0, 1, 3, 2)
    transfer = (arranged[0], arranged[1])
    norm_scale = 1.0 / (full_width * full_width)

    def spectrum(values):
        columns = columns_forward(values, outer_len, inner_len)
        stacked = jnp.stack(columns).reshape(2, extent, full_width)
        stacked = mix_forward(stacked, num_bits)
        row_part = rows_forward((stacked[0], stacked[1]), freq_offset, full_width)
        return (
            row_part[0].reshape(extent, outer_len, inner_len),
            row_part[1].reshape(extent, outer_len, inner_len),
        )

    def back_to_cells(spectral, real_only):
        flat = (spectral[0].reshape(extent, full_width), spectral[1].reshape(extent, full_width))
        row_local = rows_inverse(flat, freq_offset, full_width)
        stacked = mix_inverse(jnp.stack(row_local), num_bits)
        shaped = (
            stacked[0].reshape(extent, outer_len, inner_len),
            stacked[1].reshape(extent, outer_len, inner_len),
        )
        return columns_inverse(shaped, outer_len, inner_len, real_only)

    mask_spec = spectrum((mask_level, None))
    field_val = back_to_cells(complex_mul(transfer, mask_spec), False)
    field_val = (field_val[0] * norm_scale, field_val[1] * norm_scale)
    intensity_term = weight * (field_val[0] * field_val[0] + field_val[1] * field_val[1])
    cotangent, resist = resist_section(intensity_term, blur_taps, target, kern_count, kern_index)
    factor = 2.0 * weight * cotangent
    carried_spec = spectrum((factor * field_val[0], factor * field_val[1]))
    gradient_term = (
        back_to_cells(complex_mul((transfer[0], -transfer[1]), carried_spec), True) * norm_scale
    )
    gradient = reduce_scatter_cols(gradient_term, "kern")
    return (gradient, resist)


def solution(mesh):
    placed = (P("slab", None), P("kern", None, "slab", None), P(), P(), P(), P("slab", None))
    return jax.shard_map(
        on_device,
        mesh=mesh,
        in_specs=placed,
        out_specs=(P("slab", "kern"), P("slab", "kern")),
        check_vma=False,
    )
```

```python
import math

import jax
import jax.numpy as jnp
from jax import lax
from jax.sharding import PartitionSpec as P

CQ = 128


STEEP = 4.0
LEVEL = 0.5


def swapped(shard, axis, apart):
    return lax.ppermute(shard, axis, [(i, i ^ 1 << apart) for i in range(lax.axis_size(axis))])


def padded_2(shard, sides, width):
    for axis, dim in sides:
        devices, length = (lax.axis_size(axis), shard.shape[dim])
        up = [(i, (i + 1) % devices) for i in range(devices - 1)]
        down = [(j, i) for i, j in up]
        last = lax.slice_in_dim(shard, length - width, length, axis=dim)
        initial = lax.slice_in_dim(shard, 0, width, axis=dim)
        before = lax.ppermute(last, axis, up)
        after = lax.ppermute(initial, axis, down)
        shard = jnp.concatenate([before, shard, after], axis=dim)
    return shard


def reversed_bits(number, num_bits):
    result = number * 0
    for bit_pos in range(num_bits):
        result = result * 2 + number // 2**bit_pos % 2
    return result


def rotation(product, length, sign_val):
    fraction = (product % length).astype(jnp.float32) / length
    angles = sign_val * 2.0 * math.pi * fraction
    return (jnp.cos(angles), jnp.sin(angles))


def complex_mul(first_pair, second_pair):
    real_part = first_pair[0] * second_pair[0] - first_pair[1] * second_pair[1]
    imag_part = first_pair[0] * second_pair[1] + first_pair[1] * second_pair[0]
    return (real_part, imag_part)


def table_product(pattern, matrix, values):
    highest = lax.Precision.HIGHEST

    def single(first_op, second_op):
        return jnp.einsum(pattern, first_op, second_op, precision=highest)

    if values[1] is None:
        return (single(matrix[0], values[0]), single(matrix[1], values[0]))
    real_part = single(matrix[0], values[0]) - single(matrix[1], values[1])
    imag_part = single(matrix[0], values[1]) + single(matrix[1], values[0])
    return (real_part, imag_part)


def columns_forward(values, outer_len, inner_len):
    extent = values[0].shape[0]
    shaped = tuple(
        (None if piece is None else piece.reshape(extent, outer_len, inner_len) for piece in values)
    )
    outer_idx = jnp.arange(outer_len)
    inner_idx = jnp.arange(inner_len)
    section = table_product(
        "ab,rbq->raq", rotation(outer_idx[:, None] * outer_idx[None, :], outer_len, -1.0), shaped
    )
    section = complex_mul(
        section, rotation(outer_idx[:, None] * inner_idx[None, :], outer_len * inner_len, -1.0)
    )
    return table_product(
        "bk,rpb->rpk", rotation(inner_idx[:, None] * inner_idx[None, :], inner_len, -1.0), section
    )


def columns_inverse(values, outer_len, inner_len, real_only):
    extent = values[0].shape[0]
    outer_idx = jnp.arange(outer_len)
    inner_idx = jnp.arange(inner_len)
    section = table_product(
        "bk,rpb->rpk", rotation(inner_idx[:, None] * inner_idx[None, :], inner_len, 1.0), values
    )
    section = complex_mul(
        section, rotation(outer_idx[:, None] * inner_idx[None, :], outer_len * inner_len, 1.0)
    )
    matrix = rotation(outer_idx[:, None] * outer_idx[None, :], outer_len, 1.0)
    if real_only:
        highest = lax.Precision.HIGHEST
        real_part = jnp.einsum("ab,rbq->raq", matrix[0], section[0], precision=highest)
        real_part = real_part - jnp.einsum("ab,rbq->raq", matrix[1], section[1], precision=highest)
        return real_part.reshape(extent, outer_len * inner_len)
    result = table_product("ab,rbq->raq", matrix, section)
    return (
        result[0].reshape(extent, outer_len * inner_len),
        result[1].reshape(extent, outer_len * inner_len),
    )


def rows_forward(values, freq_offset, full_width):
    extent = values[0].shape[0]
    positions = jnp.arange(extent)
    twiddle = rotation(positions * freq_offset, full_width, -1.0)
    values = complex_mul(values, (twiddle[0][:, None], twiddle[1][:, None]))
    return table_product(
        "sr,rc->sc", rotation(positions[:, None] * positions[None, :], extent, -1.0), values
    )


def rows_inverse(values, freq_offset, full_width):
    extent = values[0].shape[0]
    positions = jnp.arange(extent)
    values = table_product(
        "rs,sc->rc", rotation(positions[:, None] * positions[None, :], extent, 1.0), values
    )
    twiddle = rotation(positions * freq_offset, full_width, 1.0)
    return complex_mul(values, (twiddle[0][:, None], twiddle[1][:, None]))


def pairs_forward(stacked, num_bits):
    slab_index = lax.axis_index("slab")
    for bit_level in range(num_bits - 1, -1, -1):
        half_span = 2**bit_level
        partner = swapped(stacked, "slab", bit_level)
        is_upper = slab_index // half_span % 2 == 1
        twiddle = rotation(slab_index % half_span, 2 * half_span, -1.0)
        lower_val = stacked + partner
        difference = partner - stacked
        upper_val = jnp.stack(complex_mul((difference[0], difference[1]), twiddle))
        stacked = jnp.where(is_upper, upper_val, lower_val)
    return stacked


def pairs_inverse(stacked, num_bits):
    slab_index = lax.axis_index("slab")
    for bit_level in range(num_bits):
        half_span = 2**bit_level
        partner = swapped(stacked, "slab", bit_level)
        is_upper = slab_index // half_span % 2 == 1
        twiddle = rotation(slab_index % half_span, 2 * half_span, 1.0)
        from_upper = jnp.where(is_upper, stacked, partner)
        from_lower = jnp.where(is_upper, partner, stacked)
        turned = jnp.stack(complex_mul((from_upper[0], from_upper[1]), twiddle))
        stacked = jnp.where(is_upper, from_lower - turned, from_lower + turned)
    return stacked


def mix_forward(stacked, num_bits):
    return pairs_forward(stacked, num_bits)


def mix_inverse(stacked, num_bits):
    return pairs_inverse(stacked, num_bits)


def tap_band(kernel_taps, rows, cols, offset):
    diff = jnp.arange(rows)[:, None] - jnp.arange(cols)[None, :] - offset
    band = jnp.zeros((rows, cols), jnp.float32)
    for tap_idx in range(kernel_taps.shape[0]):
        band = band + jnp.where(diff == tap_idx, kernel_taps[tap_idx], 0.0)
    return band


def blur_bands(kernel_taps, extent, block, margin):
    reach = (kernel_taps.shape[0] - 1) // 2
    row_band = tap_band(kernel_taps, extent + 2 * reach, extent, 0).T
    col_band = tap_band(kernel_taps, block + 2 * margin, block, margin - reach)
    return (row_band, col_band)


def smooth(padded, bands, extent, span):
    highest = lax.Precision.HIGHEST
    row_band, col_band = bands
    row_part = jnp.dot(row_band, padded, precision=highest)
    block = col_band.shape[1]
    margin = (col_band.shape[0] - block) // 2
    widened = jnp.pad(row_part, ((0, 0), (margin, margin)))
    windows = jnp.stack(
        [widened[:, j * block : j * block + block + 2 * margin] for j in range(span // block)], 1
    )
    result = jnp.einsum("rji,ib->rjb", windows, col_band, precision=highest)
    return result.reshape(extent, span)


def reduce_scatter_cols(values, axis):
    count = lax.axis_size(axis)
    num_bits = count.bit_length() - 1
    index = lax.axis_index(axis)
    extent, width = values.shape
    values = values.reshape((extent,) + (2,) * num_bits + (width // count,))
    for bit_level in range(num_bits):
        dim = num_bits - bit_level
        mine = index // 2**bit_level % 2
        keep = lax.dynamic_index_in_dim(values, mine, axis=dim, keepdims=False)
        send = lax.dynamic_index_in_dim(values, 1 - mine, axis=dim, keepdims=False)
        values = keep + swapped(send, axis, bit_level)
    return values.reshape(extent, width // count)


def all_gather_cols(values, axis):
    count = lax.axis_size(axis)
    num_bits = count.bit_length() - 1
    index = lax.axis_index(axis)
    extent, block = values.shape
    for bit_level in range(num_bits - 1, -1, -1):
        got = swapped(values, axis, bit_level)
        is_upper = index // 2**bit_level % 2 == 1
        low = jnp.where(is_upper, got, values)
        high = jnp.where(is_upper, values, got)
        values = jnp.stack([low, high], values.ndim - 1)
    return values.reshape(extent, block * count)


def resist_section(intensity_term, kernel_taps, target, kern_count, kern_index):
    reach = (kernel_taps.shape[0] - 1) // 2
    flipped = kernel_taps[::-1]
    extent, full_width = intensity_term.shape
    share_cols = full_width // kern_count

    def widen(values):
        return padded_2(values, (("slab", 0),), reach)

    bands = lax.optimization_barrier(
        (blur_bands(kernel_taps, extent, 128, 64), blur_bands(flipped, extent, 128, 64))
    )
    summed = all_gather_cols(reduce_scatter_cols(intensity_term, "kern"), "kern")
    goal_cells = target.astype(jnp.float32)
    resist = jax.nn.sigmoid(STEEP * (smooth(widen(summed), bands[0], extent, full_width) - LEVEL))
    slope_grad = 2.0 * (resist - goal_cells) * STEEP * resist * (1.0 - resist)
    cotangent = smooth(widen(slope_grad), bands[1], extent, full_width)
    return (cotangent, lax.dynamic_slice_in_dim(resist, kern_index * share_cols, share_cols, 1))


def on_device(mask_level, kernel_spectra, socs_weight, kernel_slot, blur_taps, target):
    extent, full_width = mask_level.shape
    slab_count = lax.axis_size("slab")
    kern_count = lax.axis_size("kern")
    num_bits = slab_count.bit_length() - 1
    inner_len = CQ
    outer_len = full_width // inner_len
    freq_offset = reversed_bits(lax.axis_index("slab"), num_bits)
    kern_index = lax.axis_index("kern")
    kernel_id = jnp.sum(jnp.where(jnp.arange(kernel_slot.shape[0]) == kern_index, kernel_slot, 0))
    weight = jnp.sum(jnp.where(jnp.arange(socs_weight.shape[0]) == kernel_id, socs_weight, 0.0))
    arranged = kernel_spectra[0].reshape(2, extent, inner_len, outer_len).transpose(0, 1, 3, 2)
    transfer = (arranged[0], arranged[1])
    norm_scale = 1.0 / (full_width * full_width)

    def spectrum(values):
        columns = columns_forward(values, outer_len, inner_len)
        stacked = jnp.stack(columns).reshape(2, extent, full_width)
        stacked = mix_forward(stacked, num_bits)
        row_part = rows_forward((stacked[0], stacked[1]), freq_offset, full_width)
        return (
            row_part[0].reshape(extent, outer_len, inner_len),
            row_part[1].reshape(extent, outer_len, inner_len),
        )

    def back_to_cells(spectral, real_only):
        flat = (spectral[0].reshape(extent, full_width), spectral[1].reshape(extent, full_width))
        row_local = rows_inverse(flat, freq_offset, full_width)
        stacked = mix_inverse(jnp.stack(row_local), num_bits)
        shaped = (
            stacked[0].reshape(extent, outer_len, inner_len),
            stacked[1].reshape(extent, outer_len, inner_len),
        )
        return columns_inverse(shaped, outer_len, inner_len, real_only)

    mask_spec = spectrum((mask_level, None))
    field_val = back_to_cells(complex_mul(transfer, mask_spec), False)
    field_val = (field_val[0] * norm_scale, field_val[1] * norm_scale)
    intensity_term = weight * (field_val[0] * field_val[0] + field_val[1] * field_val[1])
    cotangent, resist = resist_section(intensity_term, blur_taps, target, kern_count, kern_index)
    factor = 2.0 * weight * cotangent
    carried_spec = spectrum((factor * field_val[0], factor * field_val[1]))
    gradient_term = (
        back_to_cells(complex_mul((transfer[0], -transfer[1]), carried_spec), True) * norm_scale
    )
    gradient = reduce_scatter_cols(gradient_term, "kern")
    return (gradient, resist)


def solution(mesh):
    placed = (P("slab", None), P("kern", None, "slab", None), P(), P(), P(), P("slab", None))
    return jax.shard_map(
        on_device,
        mesh=mesh,
        in_specs=placed,
        out_specs=(P("slab", "kern"), P("slab", "kern")),
        check_vma=False,
    )
```

```python
import math

import jax
import jax.numpy as jnp
from jax import lax
from jax.sharding import PartitionSpec as P

CQ = 128


STEEP = 4.0
LEVEL = 0.5


def swapped(shard, axis, apart):
    return lax.ppermute(shard, axis, [(i, i ^ 1 << apart) for i in range(lax.axis_size(axis))])


def padded_2(shard, sides, width):
    for axis, dim in sides:
        devices, length = (lax.axis_size(axis), shard.shape[dim])
        up = [(i, (i + 1) % devices) for i in range(devices - 1)]
        down = [(j, i) for i, j in up]
        last = lax.slice_in_dim(shard, length - width, length, axis=dim)
        initial = lax.slice_in_dim(shard, 0, width, axis=dim)
        before = lax.ppermute(last, axis, up)
        after = lax.ppermute(initial, axis, down)
        shard = jnp.concatenate([before, shard, after], axis=dim)
    return shard


def reversed_bits(number, num_bits):
    result = number * 0
    for bit_pos in range(num_bits):
        result = result * 2 + number // 2**bit_pos % 2
    return result


def rotation(product, length, sign_val):
    fraction = (product % length).astype(jnp.float32) / length
    angles = sign_val * 2.0 * math.pi * fraction
    return (jnp.cos(angles), jnp.sin(angles))


def complex_mul(first_pair, second_pair):
    real_part = first_pair[0] * second_pair[0] - first_pair[1] * second_pair[1]
    imag_part = first_pair[0] * second_pair[1] + first_pair[1] * second_pair[0]
    return (real_part, imag_part)


def table_product(pattern, matrix, values):
    highest = lax.Precision.HIGHEST

    def single(first_op, second_op):
        return jnp.einsum(pattern, first_op, second_op, precision=highest)

    if values[1] is None:
        return (single(matrix[0], values[0]), single(matrix[1], values[0]))
    real_part = single(matrix[0], values[0]) - single(matrix[1], values[1])
    imag_part = single(matrix[0], values[1]) + single(matrix[1], values[0])
    return (real_part, imag_part)


def columns_forward(values, outer_len, inner_len):
    extent = values[0].shape[0]
    shaped = tuple(
        (None if piece is None else piece.reshape(extent, outer_len, inner_len) for piece in values)
    )
    outer_idx = jnp.arange(outer_len)
    inner_idx = jnp.arange(inner_len)
    section = table_product(
        "ab,rbq->raq", rotation(outer_idx[:, None] * outer_idx[None, :], outer_len, -1.0), shaped
    )
    section = complex_mul(
        section, rotation(outer_idx[:, None] * inner_idx[None, :], outer_len * inner_len, -1.0)
    )
    return table_product(
        "bk,rpb->rpk", rotation(inner_idx[:, None] * inner_idx[None, :], inner_len, -1.0), section
    )


def columns_inverse(values, outer_len, inner_len, real_only):
    extent = values[0].shape[0]
    outer_idx = jnp.arange(outer_len)
    inner_idx = jnp.arange(inner_len)
    section = table_product(
        "bk,rpb->rpk", rotation(inner_idx[:, None] * inner_idx[None, :], inner_len, 1.0), values
    )
    section = complex_mul(
        section, rotation(outer_idx[:, None] * inner_idx[None, :], outer_len * inner_len, 1.0)
    )
    matrix = rotation(outer_idx[:, None] * outer_idx[None, :], outer_len, 1.0)
    if real_only:
        highest = lax.Precision.HIGHEST
        real_part = jnp.einsum("ab,rbq->raq", matrix[0], section[0], precision=highest)
        real_part = real_part - jnp.einsum("ab,rbq->raq", matrix[1], section[1], precision=highest)
        return real_part.reshape(extent, outer_len * inner_len)
    result = table_product("ab,rbq->raq", matrix, section)
    return (
        result[0].reshape(extent, outer_len * inner_len),
        result[1].reshape(extent, outer_len * inner_len),
    )


def rows_forward(values, freq_offset, full_width):
    extent = values[0].shape[0]
    positions = jnp.arange(extent)
    twiddle = rotation(positions * freq_offset, full_width, -1.0)
    values = complex_mul(values, (twiddle[0][:, None], twiddle[1][:, None]))
    return table_product(
        "sr,rc->sc", rotation(positions[:, None] * positions[None, :], extent, -1.0), values
    )


def rows_inverse(values, freq_offset, full_width):
    extent = values[0].shape[0]
    positions = jnp.arange(extent)
    values = table_product(
        "rs,sc->rc", rotation(positions[:, None] * positions[None, :], extent, 1.0), values
    )
    twiddle = rotation(positions * freq_offset, full_width, 1.0)
    return complex_mul(values, (twiddle[0][:, None], twiddle[1][:, None]))


def pairs_forward(stacked, num_bits):
    slab_index = lax.axis_index("slab")
    for bit_level in range(num_bits - 1, -1, -1):
        half_span = 2**bit_level
        partner = swapped(stacked, "slab", bit_level)
        is_upper = slab_index // half_span % 2 == 1
        twiddle = rotation(slab_index % half_span, 2 * half_span, -1.0)
        lower_val = stacked + partner
        difference = partner - stacked
        upper_val = jnp.stack(complex_mul((difference[0], difference[1]), twiddle))
        stacked = jnp.where(is_upper, upper_val, lower_val)
    return stacked


def pairs_inverse(stacked, num_bits):
    slab_index = lax.axis_index("slab")
    for bit_level in range(num_bits):
        half_span = 2**bit_level
        partner = swapped(stacked, "slab", bit_level)
        is_upper = slab_index // half_span % 2 == 1
        twiddle = rotation(slab_index % half_span, 2 * half_span, 1.0)
        from_upper = jnp.where(is_upper, stacked, partner)
        from_lower = jnp.where(is_upper, partner, stacked)
        turned = jnp.stack(complex_mul((from_upper[0], from_upper[1]), twiddle))
        stacked = jnp.where(is_upper, from_lower - turned, from_lower + turned)
    return stacked


def mix_forward(stacked, num_bits):
    return pairs_forward(stacked, num_bits)


def mix_inverse(stacked, num_bits):
    return pairs_inverse(stacked, num_bits)


def tap_band(kernel_taps, rows, cols, offset):
    diff = jnp.arange(rows)[:, None] - jnp.arange(cols)[None, :] - offset
    tap_idx = jnp.arange(kernel_taps.shape[0])[:, None, None]
    hits = jnp.where(diff[None] == tap_idx, kernel_taps[:, None, None], 0.0)
    return jnp.sum(hits, axis=0)


def blur_bands(kernel_taps, extent, block, margin):
    reach = (kernel_taps.shape[0] - 1) // 2
    row_band = tap_band(kernel_taps, extent + 2 * reach, extent, 0).T
    col_band = tap_band(kernel_taps, block + 2 * margin, block, margin - reach)
    return (row_band, col_band)


def smooth(padded, bands, extent, span):
    highest = lax.Precision.HIGHEST
    row_band, col_band = bands
    row_part = jnp.dot(row_band, padded, precision=highest)
    block = col_band.shape[1]
    margin = (col_band.shape[0] - block) // 2
    widened = jnp.pad(row_part, ((0, 0), (margin, margin)))
    windows = jnp.stack(
        [widened[:, j * block : j * block + block + 2 * margin] for j in range(span // block)], 1
    )
    result = jnp.einsum("rji,ib->rjb", windows, col_band, precision=highest)
    return result.reshape(extent, span)


def reduce_scatter_cols(values, axis):
    count = lax.axis_size(axis)
    num_bits = count.bit_length() - 1
    index = lax.axis_index(axis)
    extent, width = values.shape
    values = values.reshape((extent,) + (2,) * num_bits + (width // count,))
    for bit_level in range(num_bits):
        dim = num_bits - bit_level
        mine = index // 2**bit_level % 2
        keep = lax.dynamic_index_in_dim(values, mine, axis=dim, keepdims=False)
        send = lax.dynamic_index_in_dim(values, 1 - mine, axis=dim, keepdims=False)
        values = keep + swapped(send, axis, bit_level)
    return values.reshape(extent, width // count)


def all_gather_cols(values, axis):
    count = lax.axis_size(axis)
    num_bits = count.bit_length() - 1
    index = lax.axis_index(axis)
    extent, block = values.shape
    for bit_level in range(num_bits - 1, -1, -1):
        got = swapped(values, axis, bit_level)
        is_upper = index // 2**bit_level % 2 == 1
        low = jnp.where(is_upper, got, values)
        high = jnp.where(is_upper, values, got)
        values = jnp.stack([low, high], values.ndim - 1)
    return values.reshape(extent, block * count)


def resist_section(intensity_term, kernel_taps, target, kern_count, kern_index):
    reach = (kernel_taps.shape[0] - 1) // 2
    flipped = kernel_taps[::-1]
    extent, full_width = intensity_term.shape
    share_cols = full_width // kern_count

    def widen(values):
        return padded_2(values, (("slab", 0),), reach)

    bands = lax.optimization_barrier(
        (blur_bands(kernel_taps, extent, 128, 64), blur_bands(flipped, extent, 128, 64))
    )
    summed = all_gather_cols(reduce_scatter_cols(intensity_term, "kern"), "kern")
    goal_cells = target.astype(jnp.float32)
    resist = jax.nn.sigmoid(STEEP * (smooth(widen(summed), bands[0], extent, full_width) - LEVEL))
    slope_grad = 2.0 * (resist - goal_cells) * STEEP * resist * (1.0 - resist)
    cotangent = smooth(widen(slope_grad), bands[1], extent, full_width)
    return (cotangent, lax.dynamic_slice_in_dim(resist, kern_index * share_cols, share_cols, 1))


def on_device(mask_level, kernel_spectra, socs_weight, kernel_slot, blur_taps, target):
    extent, full_width = mask_level.shape
    slab_count = lax.axis_size("slab")
    kern_count = lax.axis_size("kern")
    num_bits = slab_count.bit_length() - 1
    inner_len = CQ
    outer_len = full_width // inner_len
    freq_offset = reversed_bits(lax.axis_index("slab"), num_bits)
    kern_index = lax.axis_index("kern")
    kernel_id = jnp.sum(jnp.where(jnp.arange(kernel_slot.shape[0]) == kern_index, kernel_slot, 0))
    weight = jnp.sum(jnp.where(jnp.arange(socs_weight.shape[0]) == kernel_id, socs_weight, 0.0))
    arranged = kernel_spectra[0].reshape(2, extent, inner_len, outer_len).transpose(0, 1, 3, 2)
    transfer = (arranged[0], arranged[1])
    norm_scale = 1.0 / (full_width * full_width)

    def spectrum(values):
        columns = columns_forward(values, outer_len, inner_len)
        stacked = jnp.stack(columns).reshape(2, extent, full_width)
        stacked = mix_forward(stacked, num_bits)
        row_part = rows_forward((stacked[0], stacked[1]), freq_offset, full_width)
        return (
            row_part[0].reshape(extent, outer_len, inner_len),
            row_part[1].reshape(extent, outer_len, inner_len),
        )

    def back_to_cells(spectral, real_only):
        flat = (spectral[0].reshape(extent, full_width), spectral[1].reshape(extent, full_width))
        row_local = rows_inverse(flat, freq_offset, full_width)
        stacked = mix_inverse(jnp.stack(row_local), num_bits)
        shaped = (
            stacked[0].reshape(extent, outer_len, inner_len),
            stacked[1].reshape(extent, outer_len, inner_len),
        )
        return columns_inverse(shaped, outer_len, inner_len, real_only)

    mask_spec = spectrum((mask_level, None))
    field_val = back_to_cells(complex_mul(transfer, mask_spec), False)
    field_val = (field_val[0] * norm_scale, field_val[1] * norm_scale)
    intensity_term = weight * (field_val[0] * field_val[0] + field_val[1] * field_val[1])
    cotangent, resist = resist_section(intensity_term, blur_taps, target, kern_count, kern_index)
    factor = 2.0 * weight * cotangent
    carried_spec = spectrum((factor * field_val[0], factor * field_val[1]))
    gradient_term = (
        back_to_cells(complex_mul((transfer[0], -transfer[1]), carried_spec), True) * norm_scale
    )
    gradient = reduce_scatter_cols(gradient_term, "kern")
    return (gradient, resist)


def solution(mesh):
    placed = (P("slab", None), P("kern", None, "slab", None), P(), P(), P(), P("slab", None))
    return jax.shard_map(
        on_device,
        mesh=mesh,
        in_specs=placed,
        out_specs=(P("slab", "kern"), P("slab", "kern")),
        check_vma=False,
    )
```

```python
import math

import jax
import jax.numpy as jnp
from jax import lax
from jax.sharding import PartitionSpec as P

CQ = 128


STEEP = 4.0
LEVEL = 0.5


def swapped(shard, axis, apart):
    return lax.ppermute(shard, axis, [(i, i ^ 1 << apart) for i in range(lax.axis_size(axis))])


def padded_2(shard, sides, width):
    for axis, dim in sides:
        devices, length = (lax.axis_size(axis), shard.shape[dim])
        up = [(i, (i + 1) % devices) for i in range(devices - 1)]
        down = [(j, i) for i, j in up]
        last = lax.slice_in_dim(shard, length - width, length, axis=dim)
        initial = lax.slice_in_dim(shard, 0, width, axis=dim)
        before = lax.ppermute(last, axis, up)
        after = lax.ppermute(initial, axis, down)
        shard = jnp.concatenate([before, shard, after], axis=dim)
    return shard


def reversed_bits(number, num_bits):
    result = number * 0
    for bit_pos in range(num_bits):
        result = result * 2 + number // 2**bit_pos % 2
    return result


def rotation(product, length, sign_val):
    fraction = (product % length).astype(jnp.float32) / length
    angles = sign_val * 2.0 * math.pi * fraction
    return (jnp.cos(angles), jnp.sin(angles))


def complex_mul(first_pair, second_pair):
    real_part = first_pair[0] * second_pair[0] - first_pair[1] * second_pair[1]
    imag_part = first_pair[0] * second_pair[1] + first_pair[1] * second_pair[0]
    return (real_part, imag_part)


def table_product(pattern, matrix, values):
    highest = lax.Precision.HIGHEST

    def single(first_op, second_op):
        return jnp.einsum(pattern, first_op, second_op, precision=highest)

    if values[1] is None:
        return (single(matrix[0], values[0]), single(matrix[1], values[0]))
    real_part = single(matrix[0], values[0]) - single(matrix[1], values[1])
    imag_part = single(matrix[0], values[1]) + single(matrix[1], values[0])
    return (real_part, imag_part)


def columns_forward(values, outer_len, inner_len):
    extent = values[0].shape[0]
    shaped = tuple(
        (None if piece is None else piece.reshape(extent, outer_len, inner_len) for piece in values)
    )
    outer_idx = jnp.arange(outer_len)
    inner_idx = jnp.arange(inner_len)
    section = table_product(
        "ab,rbq->raq", rotation(outer_idx[:, None] * outer_idx[None, :], outer_len, -1.0), shaped
    )
    section = complex_mul(
        section, rotation(outer_idx[:, None] * inner_idx[None, :], outer_len * inner_len, -1.0)
    )
    return table_product(
        "bk,rpb->rpk", rotation(inner_idx[:, None] * inner_idx[None, :], inner_len, -1.0), section
    )


def columns_inverse(values, outer_len, inner_len, real_only):
    extent = values[0].shape[0]
    outer_idx = jnp.arange(outer_len)
    inner_idx = jnp.arange(inner_len)
    section = table_product(
        "bk,rpb->rpk", rotation(inner_idx[:, None] * inner_idx[None, :], inner_len, 1.0), values
    )
    section = complex_mul(
        section, rotation(outer_idx[:, None] * inner_idx[None, :], outer_len * inner_len, 1.0)
    )
    matrix = rotation(outer_idx[:, None] * outer_idx[None, :], outer_len, 1.0)
    if real_only:
        highest = lax.Precision.HIGHEST
        real_part = jnp.einsum("ab,rbq->raq", matrix[0], section[0], precision=highest)
        real_part = real_part - jnp.einsum("ab,rbq->raq", matrix[1], section[1], precision=highest)
        return real_part.reshape(extent, outer_len * inner_len)
    result = table_product("ab,rbq->raq", matrix, section)
    return (
        result[0].reshape(extent, outer_len * inner_len),
        result[1].reshape(extent, outer_len * inner_len),
    )


def rows_forward(values, freq_offset, full_width):
    extent = values[0].shape[0]
    positions = jnp.arange(extent)
    twiddle = rotation(positions * freq_offset, full_width, -1.0)
    values = complex_mul(values, (twiddle[0][:, None], twiddle[1][:, None]))
    return table_product(
        "sr,rc->sc", rotation(positions[:, None] * positions[None, :], extent, -1.0), values
    )


def rows_inverse(values, freq_offset, full_width):
    extent = values[0].shape[0]
    positions = jnp.arange(extent)
    values = table_product(
        "rs,sc->rc", rotation(positions[:, None] * positions[None, :], extent, 1.0), values
    )
    twiddle = rotation(positions * freq_offset, full_width, 1.0)
    return complex_mul(values, (twiddle[0][:, None], twiddle[1][:, None]))


def pairs_forward(stacked, num_bits):
    slab_index = lax.axis_index("slab")
    for bit_level in range(num_bits - 1, -1, -1):
        half_span = 2**bit_level
        partner = swapped(stacked, "slab", bit_level)
        is_upper = slab_index // half_span % 2 == 1
        twiddle = rotation(slab_index % half_span, 2 * half_span, -1.0)
        lower_val = stacked + partner
        difference = partner - stacked
        upper_val = jnp.stack(complex_mul((difference[0], difference[1]), twiddle))
        stacked = jnp.where(is_upper, upper_val, lower_val)
    return stacked


def pairs_inverse(stacked, num_bits):
    slab_index = lax.axis_index("slab")
    for bit_level in range(num_bits):
        half_span = 2**bit_level
        partner = swapped(stacked, "slab", bit_level)
        is_upper = slab_index // half_span % 2 == 1
        twiddle = rotation(slab_index % half_span, 2 * half_span, 1.0)
        from_upper = jnp.where(is_upper, stacked, partner)
        from_lower = jnp.where(is_upper, partner, stacked)
        turned = jnp.stack(complex_mul((from_upper[0], from_upper[1]), twiddle))
        stacked = jnp.where(is_upper, from_lower - turned, from_lower + turned)
    return stacked


def mix_forward(stacked, num_bits):
    return pairs_forward(stacked, num_bits)


def mix_inverse(stacked, num_bits):
    return pairs_inverse(stacked, num_bits)


def tap_band(kernel_taps, rows, cols, offset):
    diff = jnp.arange(rows)[:, None] - jnp.arange(cols)[None, :] - offset
    tap_idx = jnp.arange(kernel_taps.shape[0])[:, None, None]
    hits = jnp.where(diff[None] == tap_idx, kernel_taps[:, None, None], 0.0)
    return jnp.sum(hits, axis=0)


def blur_bands(kernel_taps, extent, block, margin):
    reach = (kernel_taps.shape[0] - 1) // 2
    row_band = tap_band(kernel_taps, extent + 2 * reach, extent, 0).T
    col_band = tap_band(kernel_taps, block + 2 * margin, block, margin - reach)
    return (row_band, col_band)


def smooth(padded, bands, extent, span):
    highest = lax.Precision.HIGHEST
    row_band, col_band = bands
    row_part = jnp.dot(row_band, padded, precision=highest)
    block = col_band.shape[1]
    margin = (col_band.shape[0] - block) // 2
    widened = jnp.pad(row_part, ((0, 0), (margin, margin)))
    windows = jnp.stack(
        [widened[:, j * block : j * block + block + 2 * margin] for j in range(span // block)], 1
    )
    result = jnp.einsum("rji,ib->rjb", windows, col_band, precision=highest)
    return result.reshape(extent, span)


def reduce_scatter_cols(values, axis):
    count = lax.axis_size(axis)
    num_bits = count.bit_length() - 1
    index = lax.axis_index(axis)
    extent, width = values.shape
    values = values.reshape((extent,) + (2,) * num_bits + (width // count,))
    for bit_level in range(num_bits):
        dim = num_bits - bit_level
        mine = index // 2**bit_level % 2
        keep = lax.dynamic_index_in_dim(values, mine, axis=dim, keepdims=False)
        send = lax.dynamic_index_in_dim(values, 1 - mine, axis=dim, keepdims=False)
        values = keep + swapped(send, axis, bit_level)
    return values.reshape(extent, width // count)


def all_gather_cols(values, axis):
    count = lax.axis_size(axis)
    num_bits = count.bit_length() - 1
    index = lax.axis_index(axis)
    extent, block = values.shape
    for bit_level in range(num_bits - 1, -1, -1):
        got = swapped(values, axis, bit_level)
        is_upper = index // 2**bit_level % 2 == 1
        low = jnp.where(is_upper, got, values)
        high = jnp.where(is_upper, values, got)
        values = jnp.stack([low, high], values.ndim - 1)
    return values.reshape(extent, block * count)


def resist_section(intensity_term, kernel_taps, target, kern_count, kern_index):
    reach = (kernel_taps.shape[0] - 1) // 2
    flipped = kernel_taps[::-1]
    extent, full_width = intensity_term.shape
    share_cols = full_width // kern_count

    def widen(values):
        return padded_2(values, (("slab", 0),), reach)

    bands = lax.optimization_barrier(
        (blur_bands(kernel_taps, extent, 128, 64), blur_bands(flipped, extent, 128, 64))
    )
    summed = all_gather_cols(reduce_scatter_cols(intensity_term, "kern"), "kern")
    goal_cells = target.astype(jnp.float32)
    resist = jax.nn.sigmoid(STEEP * (smooth(widen(summed), bands[0], extent, full_width) - LEVEL))
    slope_grad = 2.0 * (resist - goal_cells) * STEEP * resist * (1.0 - resist)
    cotangent = smooth(widen(slope_grad), bands[1], extent, full_width)
    return (cotangent, lax.dynamic_slice_in_dim(resist, kern_index * share_cols, share_cols, 1))


def to_columns(stacked):
    pieces, extent, width = stacked.shape
    count = lax.axis_size("slab")
    split = stacked.reshape(pieces, extent, count, width // count).transpose(0, 2, 1, 3)
    return lax.all_to_all(split, "slab", 1, 1, tiled=True)


def to_rows(stacked):
    pieces, count, extent, share = stacked.shape
    joined = lax.all_to_all(stacked, "slab", 1, 1, tiled=True)
    return joined.transpose(0, 2, 1, 3).reshape(pieces, extent, count * share)


def row_tables(count, extent, sign_val):
    num_bits = count.bit_length() - 1
    slab_idx = jnp.arange(count)
    local_idx = jnp.arange(extent)
    flipped = reversed_bits(slab_idx, num_bits)
    across = rotation(flipped[:, None] * slab_idx[None, :], count, sign_val)
    twiddle = rotation(flipped[:, None] * local_idx[None, :], count * extent, sign_val)
    within = rotation(local_idx[:, None] * local_idx[None, :], extent, sign_val)
    return (across, twiddle, within)


def rows_forward_t(values):
    count, extent, _ = values[0].shape
    across, twiddle, within = row_tables(count, extent, -1.0)
    values = table_product("ed,dpv->epv", across, values)
    values = complex_mul(values, (twiddle[0][:, :, None], twiddle[1][:, :, None]))
    return table_product("qp,epv->eqv", within, values)


def rows_inverse_t(values):
    count, extent, _ = values[0].shape
    across, twiddle, within = row_tables(count, extent, 1.0)
    values = table_product("pq,eqv->epv", within, values)
    values = complex_mul(values, (twiddle[0][:, :, None], twiddle[1][:, :, None]))
    return table_product("ed,epv->dpv", across, values)


def on_device(mask_level, kernel_spectra, socs_weight, kernel_slot, blur_taps, target):
    extent, full_width = mask_level.shape
    slab_count = lax.axis_size("slab")
    kern_count = lax.axis_size("kern")
    num_bits = slab_count.bit_length() - 1
    inner_len = CQ
    outer_len = full_width // inner_len
    freq_offset = reversed_bits(lax.axis_index("slab"), num_bits)
    kern_index = lax.axis_index("kern")
    kernel_id = jnp.sum(jnp.where(jnp.arange(kernel_slot.shape[0]) == kern_index, kernel_slot, 0))
    weight = jnp.sum(jnp.where(jnp.arange(socs_weight.shape[0]) == kernel_id, socs_weight, 0.0))
    arranged = kernel_spectra[0].reshape(2, extent, inner_len, outer_len).transpose(0, 1, 3, 2)
    arranged = to_columns(arranged.reshape(2, extent, full_width))
    transfer = (arranged[0], arranged[1])
    norm_scale = 1.0 / (full_width * full_width)

    def spectrum(values):
        columns = columns_forward(values, outer_len, inner_len)
        stacked = to_columns(jnp.stack(columns).reshape(2, extent, full_width))
        return rows_forward_t((stacked[0], stacked[1]))

    def back_to_cells(spectral, real_only):
        stacked = to_rows(jnp.stack(rows_inverse_t(spectral)))
        shaped = (
            stacked[0].reshape(extent, outer_len, inner_len),
            stacked[1].reshape(extent, outer_len, inner_len),
        )
        return columns_inverse(shaped, outer_len, inner_len, real_only)

    mask_spec = spectrum((mask_level, None))
    field_val = back_to_cells(complex_mul(transfer, mask_spec), False)
    field_val = (field_val[0] * norm_scale, field_val[1] * norm_scale)
    intensity_term = weight * (field_val[0] * field_val[0] + field_val[1] * field_val[1])
    cotangent, resist = resist_section(intensity_term, blur_taps, target, kern_count, kern_index)
    factor = 2.0 * weight * cotangent
    carried_spec = spectrum((factor * field_val[0], factor * field_val[1]))
    gradient_term = (
        back_to_cells(complex_mul((transfer[0], -transfer[1]), carried_spec), True) * norm_scale
    )
    gradient = reduce_scatter_cols(gradient_term, "kern")
    return (gradient, resist)


def solution(mesh):
    placed = (P("slab", None), P("kern", None, "slab", None), P(), P(), P(), P("slab", None))
    return jax.shard_map(
        on_device,
        mesh=mesh,
        in_specs=placed,
        out_specs=(P("slab", "kern"), P("slab", "kern")),
        check_vma=False,
    )
```

```python
import math

import jax
import jax.numpy as jnp
from jax import lax
from jax.sharding import PartitionSpec as P

CQ = 128


STEEP = 4.0
LEVEL = 0.5


def swapped(shard, axis, apart):
    return lax.ppermute(shard, axis, [(i, i ^ 1 << apart) for i in range(lax.axis_size(axis))])


def padded_2(shard, sides, width):
    for axis, dim in sides:
        devices, length = (lax.axis_size(axis), shard.shape[dim])
        up = [(i, (i + 1) % devices) for i in range(devices - 1)]
        down = [(j, i) for i, j in up]
        last = lax.slice_in_dim(shard, length - width, length, axis=dim)
        initial = lax.slice_in_dim(shard, 0, width, axis=dim)
        before = lax.ppermute(last, axis, up)
        after = lax.ppermute(initial, axis, down)
        shard = jnp.concatenate([before, shard, after], axis=dim)
    return shard


def reversed_bits(number, num_bits):
    result = number * 0
    for bit_pos in range(num_bits):
        result = result * 2 + number // 2**bit_pos % 2
    return result


def rotation(product, length, sign_val):
    fraction = (product % length).astype(jnp.float32) / length
    angles = sign_val * 2.0 * math.pi * fraction
    return (jnp.cos(angles), jnp.sin(angles))


def complex_mul(first_pair, second_pair):
    real_part = first_pair[0] * second_pair[0] - first_pair[1] * second_pair[1]
    imag_part = first_pair[0] * second_pair[1] + first_pair[1] * second_pair[0]
    return (real_part, imag_part)


def table_product(pattern, matrix, values):
    highest = lax.Precision.HIGHEST

    def single(first_op, second_op):
        return jnp.einsum(pattern, first_op, second_op, precision=highest)

    if values[1] is None:
        return (single(matrix[0], values[0]), single(matrix[1], values[0]))
    real_part = single(matrix[0], values[0]) - single(matrix[1], values[1])
    imag_part = single(matrix[0], values[1]) + single(matrix[1], values[0])
    return (real_part, imag_part)


def columns_forward(values, outer_len, inner_len):
    extent = values[0].shape[0]
    shaped = tuple(
        (None if piece is None else piece.reshape(extent, outer_len, inner_len) for piece in values)
    )
    outer_idx = jnp.arange(outer_len)
    inner_idx = jnp.arange(inner_len)
    section = table_product(
        "ab,rbq->raq", rotation(outer_idx[:, None] * outer_idx[None, :], outer_len, -1.0), shaped
    )
    section = complex_mul(
        section, rotation(outer_idx[:, None] * inner_idx[None, :], outer_len * inner_len, -1.0)
    )
    return table_product(
        "bk,rpb->rpk", rotation(inner_idx[:, None] * inner_idx[None, :], inner_len, -1.0), section
    )


def columns_inverse(values, outer_len, inner_len, real_only):
    extent = values[0].shape[0]
    outer_idx = jnp.arange(outer_len)
    inner_idx = jnp.arange(inner_len)
    section = table_product(
        "bk,rpb->rpk", rotation(inner_idx[:, None] * inner_idx[None, :], inner_len, 1.0), values
    )
    section = complex_mul(
        section, rotation(outer_idx[:, None] * inner_idx[None, :], outer_len * inner_len, 1.0)
    )
    matrix = rotation(outer_idx[:, None] * outer_idx[None, :], outer_len, 1.0)
    if real_only:
        highest = lax.Precision.HIGHEST
        real_part = jnp.einsum("ab,rbq->raq", matrix[0], section[0], precision=highest)
        real_part = real_part - jnp.einsum("ab,rbq->raq", matrix[1], section[1], precision=highest)
        return real_part.reshape(extent, outer_len * inner_len)
    result = table_product("ab,rbq->raq", matrix, section)
    return (
        result[0].reshape(extent, outer_len * inner_len),
        result[1].reshape(extent, outer_len * inner_len),
    )


def rows_forward(values, freq_offset, full_width):
    extent = values[0].shape[0]
    positions = jnp.arange(extent)
    twiddle = rotation(positions * freq_offset, full_width, -1.0)
    values = complex_mul(values, (twiddle[0][:, None], twiddle[1][:, None]))
    return table_product(
        "sr,rc->sc", rotation(positions[:, None] * positions[None, :], extent, -1.0), values
    )


def rows_inverse(values, freq_offset, full_width):
    extent = values[0].shape[0]
    positions = jnp.arange(extent)
    values = table_product(
        "rs,sc->rc", rotation(positions[:, None] * positions[None, :], extent, 1.0), values
    )
    twiddle = rotation(positions * freq_offset, full_width, 1.0)
    return complex_mul(values, (twiddle[0][:, None], twiddle[1][:, None]))


def pairs_forward(stacked, num_bits):
    slab_index = lax.axis_index("slab")
    for bit_level in range(num_bits - 1, -1, -1):
        half_span = 2**bit_level
        partner = swapped(stacked, "slab", bit_level)
        is_upper = slab_index // half_span % 2 == 1
        twiddle = rotation(slab_index % half_span, 2 * half_span, -1.0)
        lower_val = stacked + partner
        difference = partner - stacked
        upper_val = jnp.stack(complex_mul((difference[0], difference[1]), twiddle))
        stacked = jnp.where(is_upper, upper_val, lower_val)
    return stacked


def pairs_inverse(stacked, num_bits):
    slab_index = lax.axis_index("slab")
    for bit_level in range(num_bits):
        half_span = 2**bit_level
        partner = swapped(stacked, "slab", bit_level)
        is_upper = slab_index // half_span % 2 == 1
        twiddle = rotation(slab_index % half_span, 2 * half_span, 1.0)
        from_upper = jnp.where(is_upper, stacked, partner)
        from_lower = jnp.where(is_upper, partner, stacked)
        turned = jnp.stack(complex_mul((from_upper[0], from_upper[1]), twiddle))
        stacked = jnp.where(is_upper, from_lower - turned, from_lower + turned)
    return stacked


def mix_forward(stacked, num_bits):
    return pairs_forward(stacked, num_bits)


def mix_inverse(stacked, num_bits):
    return pairs_inverse(stacked, num_bits)


def tap_band(kernel_taps, rows, cols, offset):
    diff = jnp.arange(rows)[:, None] - jnp.arange(cols)[None, :] - offset
    tap_idx = jnp.arange(kernel_taps.shape[0])[:, None, None]
    hits = jnp.where(diff[None] == tap_idx, kernel_taps[:, None, None], 0.0)
    return jnp.sum(hits, axis=0)


def blur_bands(kernel_taps, extent, block, margin):
    reach = (kernel_taps.shape[0] - 1) // 2
    row_band = tap_band(kernel_taps, extent + 2 * reach, extent, 0).T
    col_band = tap_band(kernel_taps, block + 2 * margin, block, margin - reach)
    return (row_band, col_band)


def smooth(padded, bands, extent, span):
    highest = lax.Precision.HIGHEST
    row_band, col_band = bands
    row_part = jnp.dot(row_band, padded, precision=highest)
    block = col_band.shape[1]
    margin = (col_band.shape[0] - block) // 2
    widened = jnp.pad(row_part, ((0, 0), (margin, margin)))
    windows = jnp.stack(
        [widened[:, j * block : j * block + block + 2 * margin] for j in range(span // block)], 1
    )
    result = jnp.einsum("rji,ib->rjb", windows, col_band, precision=highest)
    return result.reshape(extent, span)


def exchanged(shard, axis, offset):
    return lax.ppermute(shard, axis, [(i, i ^ offset) for i in range(lax.axis_size(axis))])


def digit_groups(count, radix):
    groups = []
    while count > 1:
        groups.append(min(radix, count))
        count //= min(radix, count)
    return groups


def reduce_scatter_cols(values, axis, radix=4):
    count = lax.axis_size(axis)
    index = lax.axis_index(axis)
    extent, width = values.shape
    groups = digit_groups(count, radix)
    values = values.reshape((extent,) + tuple(reversed(groups)) + (width // count,))
    stride = 1
    for level, size in enumerate(groups):
        dim = len(groups) - level
        mine = index // stride % size
        total = lax.dynamic_index_in_dim(values, mine, axis=dim, keepdims=False)
        for offset in range(1, size):
            send = lax.dynamic_index_in_dim(values, mine ^ offset, axis=dim, keepdims=False)
            total = total + exchanged(send, axis, offset * stride)
        values = total
        stride *= size
    return values.reshape(extent, width // count)


def all_gather_cols(values, axis, radix=4):
    count = lax.axis_size(axis)
    index = lax.axis_index(axis)
    extent, block = values.shape
    groups = digit_groups(count, radix)
    stride = count
    for size in reversed(groups):
        stride //= size
        mine = index // stride % size
        got = [values] + [exchanged(values, axis, offset * stride) for offset in range(1, size)]
        parts = []
        for slot in range(size):
            part = jnp.zeros_like(values)
            for offset in range(size):
                part = part + jnp.where((slot ^ mine) == offset, got[offset], 0.0)
            parts.append(part)
        values = jnp.stack(parts, values.ndim - 1)
    return values.reshape(extent, block * count)


def resist_section(intensity_term, kernel_taps, target, kern_count, kern_index):
    reach = (kernel_taps.shape[0] - 1) // 2
    flipped = kernel_taps[::-1]
    extent, full_width = intensity_term.shape
    share_cols = full_width // kern_count

    def widen(values):
        return padded_2(values, (("slab", 0),), reach)

    bands = lax.optimization_barrier(
        (blur_bands(kernel_taps, extent, 128, 64), blur_bands(flipped, extent, 128, 64))
    )
    summed = all_gather_cols(reduce_scatter_cols(intensity_term, "kern"), "kern")
    goal_cells = target.astype(jnp.float32)
    resist = jax.nn.sigmoid(STEEP * (smooth(widen(summed), bands[0], extent, full_width) - LEVEL))
    slope_grad = 2.0 * (resist - goal_cells) * STEEP * resist * (1.0 - resist)
    cotangent = smooth(widen(slope_grad), bands[1], extent, full_width)
    return (cotangent, lax.dynamic_slice_in_dim(resist, kern_index * share_cols, share_cols, 1))


def to_columns(stacked):
    pieces, extent, width = stacked.shape
    count = lax.axis_size("slab")
    split = stacked.reshape(pieces, extent, count, width // count).transpose(0, 2, 1, 3)
    return lax.all_to_all(split, "slab", 1, 1, tiled=True)


def to_rows(stacked):
    pieces, count, extent, share = stacked.shape
    joined = lax.all_to_all(stacked, "slab", 1, 1, tiled=True)
    return joined.transpose(0, 2, 1, 3).reshape(pieces, extent, count * share)


def row_tables(count, extent, sign_val):
    num_bits = count.bit_length() - 1
    slab_idx = jnp.arange(count)
    local_idx = jnp.arange(extent)
    flipped = reversed_bits(slab_idx, num_bits)
    across = rotation(flipped[:, None] * slab_idx[None, :], count, sign_val)
    twiddle = rotation(flipped[:, None] * local_idx[None, :], count * extent, sign_val)
    within = rotation(local_idx[:, None] * local_idx[None, :], extent, sign_val)
    return (across, twiddle, within)


def rows_forward_t(values):
    count, extent, _ = values[0].shape
    across, twiddle, within = row_tables(count, extent, -1.0)
    values = table_product("ed,dpv->epv", across, values)
    values = complex_mul(values, (twiddle[0][:, :, None], twiddle[1][:, :, None]))
    return table_product("qp,epv->eqv", within, values)


def rows_inverse_t(values):
    count, extent, _ = values[0].shape
    across, twiddle, within = row_tables(count, extent, 1.0)
    values = table_product("pq,eqv->epv", within, values)
    values = complex_mul(values, (twiddle[0][:, :, None], twiddle[1][:, :, None]))
    return table_product("ed,epv->dpv", across, values)


def on_device(mask_level, kernel_spectra, socs_weight, kernel_slot, blur_taps, target):
    extent, full_width = mask_level.shape
    slab_count = lax.axis_size("slab")
    kern_count = lax.axis_size("kern")
    num_bits = slab_count.bit_length() - 1
    inner_len = CQ
    outer_len = full_width // inner_len
    freq_offset = reversed_bits(lax.axis_index("slab"), num_bits)
    kern_index = lax.axis_index("kern")
    kernel_id = jnp.sum(jnp.where(jnp.arange(kernel_slot.shape[0]) == kern_index, kernel_slot, 0))
    weight = jnp.sum(jnp.where(jnp.arange(socs_weight.shape[0]) == kernel_id, socs_weight, 0.0))
    arranged = kernel_spectra[0].reshape(2, extent, inner_len, outer_len).transpose(0, 1, 3, 2)
    arranged = to_columns(arranged.reshape(2, extent, full_width))
    transfer = (arranged[0], arranged[1])
    norm_scale = 1.0 / (full_width * full_width)

    def spectrum(values):
        columns = columns_forward(values, outer_len, inner_len)
        stacked = to_columns(jnp.stack(columns).reshape(2, extent, full_width))
        return rows_forward_t((stacked[0], stacked[1]))

    def back_to_cells(spectral, real_only):
        stacked = to_rows(jnp.stack(rows_inverse_t(spectral)))
        shaped = (
            stacked[0].reshape(extent, outer_len, inner_len),
            stacked[1].reshape(extent, outer_len, inner_len),
        )
        return columns_inverse(shaped, outer_len, inner_len, real_only)

    mask_spec = spectrum((mask_level, None))
    field_val = back_to_cells(complex_mul(transfer, mask_spec), False)
    field_val = (field_val[0] * norm_scale, field_val[1] * norm_scale)
    intensity_term = weight * (field_val[0] * field_val[0] + field_val[1] * field_val[1])
    cotangent, resist = resist_section(intensity_term, blur_taps, target, kern_count, kern_index)
    factor = 2.0 * weight * cotangent
    carried_spec = spectrum((factor * field_val[0], factor * field_val[1]))
    gradient_term = (
        back_to_cells(complex_mul((transfer[0], -transfer[1]), carried_spec), True) * norm_scale
    )
    gradient = reduce_scatter_cols(gradient_term, "kern")
    return (gradient, resist)


def solution(mesh):
    placed = (P("slab", None), P("kern", None, "slab", None), P(), P(), P(), P("slab", None))
    return jax.shard_map(
        on_device,
        mesh=mesh,
        in_specs=placed,
        out_specs=(P("slab", "kern"), P("slab", "kern")),
        check_vma=False,
    )
```

```python
import math

import jax
import jax.numpy as jnp
from jax import lax
from jax.sharding import PartitionSpec as P

CQ = 128


STEEP = 4.0
LEVEL = 0.5


def swapped(shard, axis, apart):
    return lax.ppermute(shard, axis, [(i, i ^ 1 << apart) for i in range(lax.axis_size(axis))])


def padded_2(shard, sides, width):
    for axis, dim in sides:
        devices, length = (lax.axis_size(axis), shard.shape[dim])
        up = [(i, (i + 1) % devices) for i in range(devices - 1)]
        down = [(j, i) for i, j in up]
        last = lax.slice_in_dim(shard, length - width, length, axis=dim)
        initial = lax.slice_in_dim(shard, 0, width, axis=dim)
        before = lax.ppermute(last, axis, up)
        after = lax.ppermute(initial, axis, down)
        shard = jnp.concatenate([before, shard, after], axis=dim)
    return shard


def reversed_bits(number, num_bits):
    result = number * 0
    for bit_pos in range(num_bits):
        result = result * 2 + number // 2**bit_pos % 2
    return result


def rotation(product, length, sign_val):
    fraction = (product % length).astype(jnp.float32) / length
    angles = sign_val * 2.0 * math.pi * fraction
    return (jnp.cos(angles), jnp.sin(angles))


def complex_mul(first_pair, second_pair):
    real_part = first_pair[0] * second_pair[0] - first_pair[1] * second_pair[1]
    imag_part = first_pair[0] * second_pair[1] + first_pair[1] * second_pair[0]
    return (real_part, imag_part)


def table_product(pattern, matrix, values):
    highest = lax.Precision.HIGHEST

    def single(first_op, second_op):
        return jnp.einsum(pattern, first_op, second_op, precision=highest)

    if values[1] is None:
        return (single(matrix[0], values[0]), single(matrix[1], values[0]))
    real_part = single(matrix[0], values[0]) - single(matrix[1], values[1])
    imag_part = single(matrix[0], values[1]) + single(matrix[1], values[0])
    return (real_part, imag_part)


def columns_forward(values, outer_len, inner_len):
    extent = values[0].shape[0]
    shaped = tuple(
        (None if piece is None else piece.reshape(extent, outer_len, inner_len) for piece in values)
    )
    outer_idx = jnp.arange(outer_len)
    inner_idx = jnp.arange(inner_len)
    section = table_product(
        "ab,rbq->raq", rotation(outer_idx[:, None] * outer_idx[None, :], outer_len, -1.0), shaped
    )
    section = complex_mul(
        section, rotation(outer_idx[:, None] * inner_idx[None, :], outer_len * inner_len, -1.0)
    )
    return table_product(
        "bk,rpb->rpk", rotation(inner_idx[:, None] * inner_idx[None, :], inner_len, -1.0), section
    )


def columns_inverse(values, outer_len, inner_len, real_only):
    extent = values[0].shape[0]
    outer_idx = jnp.arange(outer_len)
    inner_idx = jnp.arange(inner_len)
    section = table_product(
        "bk,rpb->rpk", rotation(inner_idx[:, None] * inner_idx[None, :], inner_len, 1.0), values
    )
    section = complex_mul(
        section, rotation(outer_idx[:, None] * inner_idx[None, :], outer_len * inner_len, 1.0)
    )
    matrix = rotation(outer_idx[:, None] * outer_idx[None, :], outer_len, 1.0)
    if real_only:
        highest = lax.Precision.HIGHEST
        real_part = jnp.einsum("ab,rbq->raq", matrix[0], section[0], precision=highest)
        real_part = real_part - jnp.einsum("ab,rbq->raq", matrix[1], section[1], precision=highest)
        return real_part.reshape(extent, outer_len * inner_len)
    result = table_product("ab,rbq->raq", matrix, section)
    return (
        result[0].reshape(extent, outer_len * inner_len),
        result[1].reshape(extent, outer_len * inner_len),
    )


def rows_forward(values, freq_offset, full_width):
    extent = values[0].shape[0]
    positions = jnp.arange(extent)
    twiddle = rotation(positions * freq_offset, full_width, -1.0)
    values = complex_mul(values, (twiddle[0][:, None], twiddle[1][:, None]))
    return table_product(
        "sr,rc->sc", rotation(positions[:, None] * positions[None, :], extent, -1.0), values
    )


def rows_inverse(values, freq_offset, full_width):
    extent = values[0].shape[0]
    positions = jnp.arange(extent)
    values = table_product(
        "rs,sc->rc", rotation(positions[:, None] * positions[None, :], extent, 1.0), values
    )
    twiddle = rotation(positions * freq_offset, full_width, 1.0)
    return complex_mul(values, (twiddle[0][:, None], twiddle[1][:, None]))


def pairs_forward(stacked, num_bits):
    slab_index = lax.axis_index("slab")
    for bit_level in range(num_bits - 1, -1, -1):
        half_span = 2**bit_level
        partner = swapped(stacked, "slab", bit_level)
        is_upper = slab_index // half_span % 2 == 1
        twiddle = rotation(slab_index % half_span, 2 * half_span, -1.0)
        lower_val = stacked + partner
        difference = partner - stacked
        upper_val = jnp.stack(complex_mul((difference[0], difference[1]), twiddle))
        stacked = jnp.where(is_upper, upper_val, lower_val)
    return stacked


def pairs_inverse(stacked, num_bits):
    slab_index = lax.axis_index("slab")
    for bit_level in range(num_bits):
        half_span = 2**bit_level
        partner = swapped(stacked, "slab", bit_level)
        is_upper = slab_index // half_span % 2 == 1
        twiddle = rotation(slab_index % half_span, 2 * half_span, 1.0)
        from_upper = jnp.where(is_upper, stacked, partner)
        from_lower = jnp.where(is_upper, partner, stacked)
        turned = jnp.stack(complex_mul((from_upper[0], from_upper[1]), twiddle))
        stacked = jnp.where(is_upper, from_lower - turned, from_lower + turned)
    return stacked


def mix_forward(stacked, num_bits):
    return pairs_forward(stacked, num_bits)


def mix_inverse(stacked, num_bits):
    return pairs_inverse(stacked, num_bits)


def tap_band(kernel_taps, rows, cols, offset):
    diff = jnp.arange(rows)[:, None] - jnp.arange(cols)[None, :] - offset
    tap_idx = jnp.arange(kernel_taps.shape[0])[:, None, None]
    hits = jnp.where(diff[None] == tap_idx, kernel_taps[:, None, None], 0.0)
    return jnp.sum(hits, axis=0)


def blur_bands(kernel_taps, extent, block, margin):
    reach = (kernel_taps.shape[0] - 1) // 2
    row_band = tap_band(kernel_taps, extent + 2 * reach, extent, 0).T
    col_band = tap_band(kernel_taps, block + 2 * margin, block, margin - reach)
    return (row_band, col_band)


def smooth(padded, bands, extent, span):
    highest = lax.Precision.HIGHEST
    row_band, col_band = bands
    row_part = jnp.dot(row_band, padded, precision=highest)
    block = col_band.shape[1]
    margin = (col_band.shape[0] - block) // 2
    widened = jnp.pad(row_part, ((0, 0), (margin, margin)))
    windows = jnp.stack(
        [widened[:, j * block : j * block + block + 2 * margin] for j in range(span // block)], 1
    )
    result = jnp.einsum("rji,ib->rjb", windows, col_band, precision=highest)
    return result.reshape(extent, span)


def exchanged(shard, axis, offset):
    return lax.ppermute(shard, axis, [(i, i ^ offset) for i in range(lax.axis_size(axis))])


def digit_groups(count, radix):
    groups = []
    while count > 1:
        groups.append(min(radix, count))
        count //= min(radix, count)
    return groups


def reduce_scatter_cols(values, axis, radix=4):
    count = lax.axis_size(axis)
    index = lax.axis_index(axis)
    extent, width = values.shape
    groups = digit_groups(count, radix)
    values = values.reshape((extent,) + tuple(reversed(groups)) + (width // count,))
    stride = 1
    for level, size in enumerate(groups):
        dim = len(groups) - level
        mine = index // stride % size
        total = lax.dynamic_index_in_dim(values, mine, axis=dim, keepdims=False)
        for offset in range(1, size):
            send = lax.dynamic_index_in_dim(values, mine ^ offset, axis=dim, keepdims=False)
            total = total + exchanged(send, axis, offset * stride)
        values = total
        stride *= size
    return values.reshape(extent, width // count)


def all_gather_cols(values, axis, radix=4):
    count = lax.axis_size(axis)
    index = lax.axis_index(axis)
    extent, block = values.shape
    groups = digit_groups(count, radix)
    stride = count
    for size in reversed(groups):
        stride //= size
        mine = index // stride % size
        got = [values] + [exchanged(values, axis, offset * stride) for offset in range(1, size)]
        parts = []
        for slot in range(size):
            part = jnp.zeros_like(values)
            for offset in range(size):
                part = part + jnp.where((slot ^ mine) == offset, got[offset], 0.0)
            parts.append(part)
        values = jnp.stack(parts, values.ndim - 1)
    return values.reshape(extent, block * count)


def resist_section(intensity_term, kernel_taps, target, kern_count, kern_index):
    reach = (kernel_taps.shape[0] - 1) // 2
    flipped = kernel_taps[::-1]
    extent, full_width = intensity_term.shape
    share_cols = full_width // kern_count
    wide = extent + 2 * reach
    bands = lax.optimization_barrier(
        (blur_bands(kernel_taps, wide, 128, 64), blur_bands(flipped, extent, 128, 64))
    )
    goal_cells = padded_2(target, (("slab", 0),), reach).astype(jnp.float32)
    block = reduce_scatter_cols(intensity_term, "kern")
    summed = all_gather_cols(padded_2(block, (("slab", 0),), 2 * reach), "kern")
    resist = jax.nn.sigmoid(STEEP * (smooth(summed, bands[0], wide, full_width) - LEVEL))
    first_row = lax.axis_index("slab") * extent - reach
    rows = first_row + jnp.arange(wide)
    inside = (rows >= 0) & (rows < lax.axis_size("slab") * extent)
    slope_grad = 2.0 * (resist - goal_cells) * STEEP * resist * (1.0 - resist)
    slope_grad = jnp.where(inside[:, None], slope_grad, 0.0)
    cotangent = smooth(slope_grad, bands[1], extent, full_width)
    resist = lax.dynamic_slice_in_dim(resist[reach : reach + extent], kern_index * share_cols, share_cols, 1)
    return (cotangent, resist)


def to_columns(stacked):
    pieces, extent, width = stacked.shape
    count = lax.axis_size("slab")
    split = stacked.reshape(pieces, extent, count, width // count).transpose(0, 2, 1, 3)
    return lax.all_to_all(split, "slab", 1, 1, tiled=True)


def to_rows(stacked):
    pieces, count, extent, share = stacked.shape
    joined = lax.all_to_all(stacked, "slab", 1, 1, tiled=True)
    return joined.transpose(0, 2, 1, 3).reshape(pieces, extent, count * share)


def row_tables(count, extent, sign_val):
    num_bits = count.bit_length() - 1
    slab_idx = jnp.arange(count)
    local_idx = jnp.arange(extent)
    flipped = reversed_bits(slab_idx, num_bits)
    across = rotation(flipped[:, None] * slab_idx[None, :], count, sign_val)
    twiddle = rotation(flipped[:, None] * local_idx[None, :], count * extent, sign_val)
    within = rotation(local_idx[:, None] * local_idx[None, :], extent, sign_val)
    return (across, twiddle, within)


def rows_forward_t(values):
    count, extent, _ = values[0].shape
    across, twiddle, within = row_tables(count, extent, -1.0)
    values = table_product("ed,dpv->epv", across, values)
    values = complex_mul(values, (twiddle[0][:, :, None], twiddle[1][:, :, None]))
    return table_product("qp,epv->eqv", within, values)


def rows_inverse_t(values):
    count, extent, _ = values[0].shape
    across, twiddle, within = row_tables(count, extent, 1.0)
    values = table_product("pq,eqv->epv", within, values)
    values = complex_mul(values, (twiddle[0][:, :, None], twiddle[1][:, :, None]))
    return table_product("ed,epv->dpv", across, values)


def on_device(mask_level, kernel_spectra, socs_weight, kernel_slot, blur_taps, target):
    extent, full_width = mask_level.shape
    slab_count = lax.axis_size("slab")
    kern_count = lax.axis_size("kern")
    num_bits = slab_count.bit_length() - 1
    inner_len = CQ
    outer_len = full_width // inner_len
    freq_offset = reversed_bits(lax.axis_index("slab"), num_bits)
    kern_index = lax.axis_index("kern")
    kernel_id = jnp.sum(jnp.where(jnp.arange(kernel_slot.shape[0]) == kern_index, kernel_slot, 0))
    weight = jnp.sum(jnp.where(jnp.arange(socs_weight.shape[0]) == kernel_id, socs_weight, 0.0))
    arranged = kernel_spectra[0].reshape(2, extent, inner_len, outer_len).transpose(0, 1, 3, 2)
    arranged = to_columns(arranged.reshape(2, extent, full_width))
    transfer = (arranged[0], arranged[1])
    norm_scale = 1.0 / (full_width * full_width)

    def spectrum(values):
        columns = columns_forward(values, outer_len, inner_len)
        stacked = to_columns(jnp.stack(columns).reshape(2, extent, full_width))
        return rows_forward_t((stacked[0], stacked[1]))

    def back_to_cells(spectral, real_only):
        stacked = to_rows(jnp.stack(rows_inverse_t(spectral)))
        shaped = (
            stacked[0].reshape(extent, outer_len, inner_len),
            stacked[1].reshape(extent, outer_len, inner_len),
        )
        return columns_inverse(shaped, outer_len, inner_len, real_only)

    mask_spec = spectrum((mask_level, None))
    field_val = back_to_cells(complex_mul(transfer, mask_spec), False)
    field_val = (field_val[0] * norm_scale, field_val[1] * norm_scale)
    intensity_term = weight * (field_val[0] * field_val[0] + field_val[1] * field_val[1])
    cotangent, resist = resist_section(intensity_term, blur_taps, target, kern_count, kern_index)
    factor = 2.0 * weight * cotangent
    carried_spec = spectrum((factor * field_val[0], factor * field_val[1]))
    gradient_term = (
        back_to_cells(complex_mul((transfer[0], -transfer[1]), carried_spec), True) * norm_scale
    )
    gradient = reduce_scatter_cols(gradient_term, "kern")
    return (gradient, resist)


def solution(mesh):
    placed = (P("slab", None), P("kern", None, "slab", None), P(), P(), P(), P("slab", None))
    return jax.shard_map(
        on_device,
        mesh=mesh,
        in_specs=placed,
        out_specs=(P("slab", "kern"), P("slab", "kern")),
        check_vma=False,
    )
```

```python
import math

import jax
import jax.numpy as jnp
from jax import lax
from jax.sharding import PartitionSpec as P

CQ = 128


STEEP = 4.0
LEVEL = 0.5


def swapped(shard, axis, apart):
    return lax.ppermute(shard, axis, [(i, i ^ 1 << apart) for i in range(lax.axis_size(axis))])


def padded_2(shard, sides, width):
    for axis, dim in sides:
        devices, length = (lax.axis_size(axis), shard.shape[dim])
        up = [(i, (i + 1) % devices) for i in range(devices - 1)]
        down = [(j, i) for i, j in up]
        last = lax.slice_in_dim(shard, length - width, length, axis=dim)
        initial = lax.slice_in_dim(shard, 0, width, axis=dim)
        before = lax.ppermute(last, axis, up)
        after = lax.ppermute(initial, axis, down)
        shard = jnp.concatenate([before, shard, after], axis=dim)
    return shard


def reversed_bits(number, num_bits):
    result = number * 0
    for bit_pos in range(num_bits):
        result = result * 2 + number // 2**bit_pos % 2
    return result


def rotation(product, length, sign_val):
    fraction = (product % length).astype(jnp.float32) / length
    angles = sign_val * 2.0 * math.pi * fraction
    return (jnp.cos(angles), jnp.sin(angles))


def complex_mul(first_pair, second_pair):
    real_part = first_pair[0] * second_pair[0] - first_pair[1] * second_pair[1]
    imag_part = first_pair[0] * second_pair[1] + first_pair[1] * second_pair[0]
    return (real_part, imag_part)


def table_product(pattern, matrix, values):
    highest = lax.Precision.HIGHEST

    def single(first_op, second_op):
        return jnp.einsum(pattern, first_op, second_op, precision=highest)

    if values[1] is None:
        return (single(matrix[0], values[0]), single(matrix[1], values[0]))
    real_part = single(matrix[0], values[0]) - single(matrix[1], values[1])
    imag_part = single(matrix[0], values[1]) + single(matrix[1], values[0])
    return (real_part, imag_part)


def columns_forward(values, outer_len, inner_len):
    extent = values[0].shape[0]
    shaped = tuple(
        (None if piece is None else piece.reshape(extent, outer_len, inner_len) for piece in values)
    )
    outer_idx = jnp.arange(outer_len)
    inner_idx = jnp.arange(inner_len)
    section = table_product(
        "ab,rbq->raq", rotation(outer_idx[:, None] * outer_idx[None, :], outer_len, -1.0), shaped
    )
    section = complex_mul(
        section, rotation(outer_idx[:, None] * inner_idx[None, :], outer_len * inner_len, -1.0)
    )
    return table_product(
        "bk,rpb->rpk", rotation(inner_idx[:, None] * inner_idx[None, :], inner_len, -1.0), section
    )


def columns_inverse(values, outer_len, inner_len, real_only):
    extent = values[0].shape[0]
    outer_idx = jnp.arange(outer_len)
    inner_idx = jnp.arange(inner_len)
    section = table_product(
        "bk,rpb->rpk", rotation(inner_idx[:, None] * inner_idx[None, :], inner_len, 1.0), values
    )
    section = complex_mul(
        section, rotation(outer_idx[:, None] * inner_idx[None, :], outer_len * inner_len, 1.0)
    )
    matrix = rotation(outer_idx[:, None] * outer_idx[None, :], outer_len, 1.0)
    if real_only:
        highest = lax.Precision.HIGHEST
        real_part = jnp.einsum("ab,rbq->raq", matrix[0], section[0], precision=highest)
        real_part = real_part - jnp.einsum("ab,rbq->raq", matrix[1], section[1], precision=highest)
        return real_part.reshape(extent, outer_len * inner_len)
    result = table_product("ab,rbq->raq", matrix, section)
    return (
        result[0].reshape(extent, outer_len * inner_len),
        result[1].reshape(extent, outer_len * inner_len),
    )


def rows_forward(values, freq_offset, full_width):
    extent = values[0].shape[0]
    positions = jnp.arange(extent)
    twiddle = rotation(positions * freq_offset, full_width, -1.0)
    values = complex_mul(values, (twiddle[0][:, None], twiddle[1][:, None]))
    return table_product(
        "sr,rc->sc", rotation(positions[:, None] * positions[None, :], extent, -1.0), values
    )


def rows_inverse(values, freq_offset, full_width):
    extent = values[0].shape[0]
    positions = jnp.arange(extent)
    values = table_product(
        "rs,sc->rc", rotation(positions[:, None] * positions[None, :], extent, 1.0), values
    )
    twiddle = rotation(positions * freq_offset, full_width, 1.0)
    return complex_mul(values, (twiddle[0][:, None], twiddle[1][:, None]))


def pairs_forward(stacked, num_bits):
    slab_index = lax.axis_index("slab")
    for bit_level in range(num_bits - 1, -1, -1):
        half_span = 2**bit_level
        partner = swapped(stacked, "slab", bit_level)
        is_upper = slab_index // half_span % 2 == 1
        twiddle = rotation(slab_index % half_span, 2 * half_span, -1.0)
        lower_val = stacked + partner
        difference = partner - stacked
        upper_val = jnp.stack(complex_mul((difference[0], difference[1]), twiddle))
        stacked = jnp.where(is_upper, upper_val, lower_val)
    return stacked


def pairs_inverse(stacked, num_bits):
    slab_index = lax.axis_index("slab")
    for bit_level in range(num_bits):
        half_span = 2**bit_level
        partner = swapped(stacked, "slab", bit_level)
        is_upper = slab_index // half_span % 2 == 1
        twiddle = rotation(slab_index % half_span, 2 * half_span, 1.0)
        from_upper = jnp.where(is_upper, stacked, partner)
        from_lower = jnp.where(is_upper, partner, stacked)
        turned = jnp.stack(complex_mul((from_upper[0], from_upper[1]), twiddle))
        stacked = jnp.where(is_upper, from_lower - turned, from_lower + turned)
    return stacked


def mix_forward(stacked, num_bits):
    return pairs_forward(stacked, num_bits)


def mix_inverse(stacked, num_bits):
    return pairs_inverse(stacked, num_bits)


def tap_band(kernel_taps, rows, cols, offset):
    diff = jnp.arange(rows)[:, None] - jnp.arange(cols)[None, :] - offset
    tap_idx = jnp.arange(kernel_taps.shape[0])[:, None, None]
    hits = jnp.where(diff[None] == tap_idx, kernel_taps[:, None, None], 0.0)
    return jnp.sum(hits, axis=0)


def blur_bands(kernel_taps, extent, block, margin):
    reach = (kernel_taps.shape[0] - 1) // 2
    row_band = tap_band(kernel_taps, extent + 2 * reach, extent, 0).T
    col_band = tap_band(kernel_taps, block + 2 * margin, block, margin - reach)
    return (row_band, col_band)


def smooth(padded, bands, extent, span):
    highest = lax.Precision.HIGHEST
    row_band, col_band = bands
    row_part = jnp.dot(row_band, padded, precision=highest)
    block = col_band.shape[1]
    margin = (col_band.shape[0] - block) // 2
    widened = jnp.pad(row_part, ((0, 0), (margin, margin)))
    windows = jnp.stack(
        [widened[:, j * block : j * block + block + 2 * margin] for j in range(span // block)], 1
    )
    result = jnp.einsum("rji,ib->rjb", windows, col_band, precision=highest)
    return result.reshape(extent, span)


def exchanged(shard, axis, offset):
    return lax.ppermute(shard, axis, [(i, i ^ offset) for i in range(lax.axis_size(axis))])


def digit_groups(count, radix):
    groups = []
    while count > 1:
        groups.append(min(radix, count))
        count //= min(radix, count)
    return groups


def reduce_scatter_cols(values, axis, radix=4):
    count = lax.axis_size(axis)
    index = lax.axis_index(axis)
    extent, width = values.shape
    groups = digit_groups(count, radix)
    values = values.reshape((extent,) + tuple(reversed(groups)) + (width // count,))
    stride = 1
    for level, size in enumerate(groups):
        dim = len(groups) - level
        mine = index // stride % size
        total = lax.dynamic_index_in_dim(values, mine, axis=dim, keepdims=False)
        for offset in range(1, size):
            send = lax.dynamic_index_in_dim(values, mine ^ offset, axis=dim, keepdims=False)
            total = total + exchanged(send, axis, offset * stride)
        values = total
        stride *= size
    return values.reshape(extent, width // count)


def all_gather_cols(values, axis, radix=4):
    count = lax.axis_size(axis)
    index = lax.axis_index(axis)
    extent, block = values.shape
    groups = digit_groups(count, radix)
    stride = count
    for size in reversed(groups):
        stride //= size
        mine = index // stride % size
        got = [values] + [exchanged(values, axis, offset * stride) for offset in range(1, size)]
        parts = []
        for slot in range(size):
            part = jnp.zeros_like(values)
            for offset in range(size):
                part = part + jnp.where((slot ^ mine) == offset, got[offset], 0.0)
            parts.append(part)
        values = jnp.stack(parts, values.ndim - 1)
    return values.reshape(extent, block * count)


def all_reduce_cols(values, axis, widen, radix=4):
    count = lax.axis_size(axis)
    index = lax.axis_index(axis)
    low = min(radix, count)
    high = count // low
    extent, width = values.shape
    values = values.reshape(extent, high, low, width // count)
    mine = index % low
    total = lax.dynamic_index_in_dim(values, mine, axis=2, keepdims=False)
    for offset in range(1, low):
        send = lax.dynamic_index_in_dim(values, mine ^ offset, axis=2, keepdims=False)
        total = total + exchanged(send, axis, offset)
    upper = index // low
    got = [total] + [exchanged(total, axis, offset * low) for offset in range(1, high)]
    summed = jnp.zeros_like(total)
    for slot in range(high):
        term = jnp.zeros_like(total)
        for offset in range(high):
            term = term + jnp.where((slot ^ upper) == offset, got[offset], 0.0)
        summed = summed + term
    summed = widen(summed)
    got = [summed] + [exchanged(summed, axis, offset) for offset in range(1, low)]
    parts = []
    for slot in range(low):
        part = jnp.zeros_like(summed)
        for offset in range(low):
            part = part + jnp.where((slot ^ mine) == offset, got[offset], 0.0)
        parts.append(part)
    return jnp.stack(parts, 2).reshape(summed.shape[0], width)


def resist_section(intensity_term, kernel_taps, target, kern_count, kern_index):
    reach = (kernel_taps.shape[0] - 1) // 2
    flipped = kernel_taps[::-1]
    extent, full_width = intensity_term.shape
    share_cols = full_width // kern_count
    wide = extent + 2 * reach
    bands = lax.optimization_barrier(
        (blur_bands(kernel_taps, wide, 128, 64), blur_bands(flipped, extent, 128, 64))
    )
    goal_cells = padded_2(target, (("slab", 0),), reach).astype(jnp.float32)
    summed = all_reduce_cols(
        intensity_term, "kern", lambda block: padded_2(block, (("slab", 0),), 2 * reach)
    )
    resist = jax.nn.sigmoid(STEEP * (smooth(summed, bands[0], wide, full_width) - LEVEL))
    first_row = lax.axis_index("slab") * extent - reach
    rows = first_row + jnp.arange(wide)
    inside = (rows >= 0) & (rows < lax.axis_size("slab") * extent)
    slope_grad = 2.0 * (resist - goal_cells) * STEEP * resist * (1.0 - resist)
    slope_grad = jnp.where(inside[:, None], slope_grad, 0.0)
    cotangent = smooth(slope_grad, bands[1], extent, full_width)
    resist = lax.dynamic_slice_in_dim(resist[reach : reach + extent], kern_index * share_cols, share_cols, 1)
    return (cotangent, resist)


def to_columns(stacked):
    pieces, extent, width = stacked.shape
    count = lax.axis_size("slab")
    split = stacked.reshape(pieces, extent, count, width // count).transpose(0, 2, 1, 3)
    return lax.all_to_all(split, "slab", 1, 1, tiled=True)


def to_rows(stacked):
    pieces, count, extent, share = stacked.shape
    joined = lax.all_to_all(stacked, "slab", 1, 1, tiled=True)
    return joined.transpose(0, 2, 1, 3).reshape(pieces, extent, count * share)


def row_tables(count, extent, sign_val):
    num_bits = count.bit_length() - 1
    slab_idx = jnp.arange(count)
    local_idx = jnp.arange(extent)
    flipped = reversed_bits(slab_idx, num_bits)
    across = rotation(flipped[:, None] * slab_idx[None, :], count, sign_val)
    twiddle = rotation(flipped[:, None] * local_idx[None, :], count * extent, sign_val)
    within = rotation(local_idx[:, None] * local_idx[None, :], extent, sign_val)
    return (across, twiddle, within)


def rows_forward_t(values):
    count, extent, _ = values[0].shape
    across, twiddle, within = row_tables(count, extent, -1.0)
    values = table_product("ed,dpv->epv", across, values)
    values = complex_mul(values, (twiddle[0][:, :, None], twiddle[1][:, :, None]))
    return table_product("qp,epv->eqv", within, values)


def rows_inverse_t(values):
    count, extent, _ = values[0].shape
    across, twiddle, within = row_tables(count, extent, 1.0)
    values = table_product("pq,eqv->epv", within, values)
    values = complex_mul(values, (twiddle[0][:, :, None], twiddle[1][:, :, None]))
    return table_product("ed,epv->dpv", across, values)


def on_device(mask_level, kernel_spectra, socs_weight, kernel_slot, blur_taps, target):
    extent, full_width = mask_level.shape
    slab_count = lax.axis_size("slab")
    kern_count = lax.axis_size("kern")
    num_bits = slab_count.bit_length() - 1
    inner_len = CQ
    outer_len = full_width // inner_len
    freq_offset = reversed_bits(lax.axis_index("slab"), num_bits)
    kern_index = lax.axis_index("kern")
    kernel_id = jnp.sum(jnp.where(jnp.arange(kernel_slot.shape[0]) == kern_index, kernel_slot, 0))
    weight = jnp.sum(jnp.where(jnp.arange(socs_weight.shape[0]) == kernel_id, socs_weight, 0.0))
    arranged = kernel_spectra[0].reshape(2, extent, inner_len, outer_len).transpose(0, 1, 3, 2)
    arranged = to_columns(arranged.reshape(2, extent, full_width))
    transfer = (arranged[0], arranged[1])
    norm_scale = 1.0 / (full_width * full_width)

    def spectrum(values):
        columns = columns_forward(values, outer_len, inner_len)
        stacked = to_columns(jnp.stack(columns).reshape(2, extent, full_width))
        return rows_forward_t((stacked[0], stacked[1]))

    def back_to_cells(spectral, real_only):
        stacked = to_rows(jnp.stack(rows_inverse_t(spectral)))
        shaped = (
            stacked[0].reshape(extent, outer_len, inner_len),
            stacked[1].reshape(extent, outer_len, inner_len),
        )
        return columns_inverse(shaped, outer_len, inner_len, real_only)

    mask_spec = spectrum((mask_level, None))
    field_val = back_to_cells(complex_mul(transfer, mask_spec), False)
    field_val = (field_val[0] * norm_scale, field_val[1] * norm_scale)
    intensity_term = weight * (field_val[0] * field_val[0] + field_val[1] * field_val[1])
    cotangent, resist = resist_section(intensity_term, blur_taps, target, kern_count, kern_index)
    factor = 2.0 * weight * cotangent
    carried_spec = spectrum((factor * field_val[0], factor * field_val[1]))
    gradient_term = (
        back_to_cells(complex_mul((transfer[0], -transfer[1]), carried_spec), True) * norm_scale
    )
    gradient = reduce_scatter_cols(gradient_term, "kern")
    return (gradient, resist)


def solution(mesh):
    placed = (P("slab", None), P("kern", None, "slab", None), P(), P(), P(), P("slab", None))
    return jax.shard_map(
        on_device,
        mesh=mesh,
        in_specs=placed,
        out_specs=(P("slab", "kern"), P("slab", "kern")),
        check_vma=False,
    )
```

```python
import math

import jax
import jax.numpy as jnp
from jax import lax
from jax.sharding import PartitionSpec as P

CQ = 128


STEEP = 4.0
LEVEL = 0.5


def swapped(shard, axis, apart):
    return lax.ppermute(shard, axis, [(i, i ^ 1 << apart) for i in range(lax.axis_size(axis))])


def padded_2(shard, sides, width):
    for axis, dim in sides:
        devices, length = (lax.axis_size(axis), shard.shape[dim])
        up = [(i, (i + 1) % devices) for i in range(devices - 1)]
        down = [(j, i) for i, j in up]
        last = lax.slice_in_dim(shard, length - width, length, axis=dim)
        initial = lax.slice_in_dim(shard, 0, width, axis=dim)
        before = lax.ppermute(last, axis, up)
        after = lax.ppermute(initial, axis, down)
        shard = jnp.concatenate([before, shard, after], axis=dim)
    return shard


def reversed_bits(number, num_bits):
    result = number * 0
    for bit_pos in range(num_bits):
        result = result * 2 + number // 2**bit_pos % 2
    return result


def rotation(product, length, sign_val):
    fraction = (product % length).astype(jnp.float32) / length
    angles = sign_val * 2.0 * math.pi * fraction
    return (jnp.cos(angles), jnp.sin(angles))


def complex_mul(first_pair, second_pair):
    real_part = first_pair[0] * second_pair[0] - first_pair[1] * second_pair[1]
    imag_part = first_pair[0] * second_pair[1] + first_pair[1] * second_pair[0]
    return (real_part, imag_part)


def table_product(pattern, matrix, values):
    highest = lax.Precision.HIGHEST

    def single(first_op, second_op):
        return jnp.einsum(pattern, first_op, second_op, precision=highest)

    if values[1] is None:
        return (single(matrix[0], values[0]), single(matrix[1], values[0]))
    real_part = single(matrix[0], values[0]) - single(matrix[1], values[1])
    imag_part = single(matrix[0], values[1]) + single(matrix[1], values[0])
    return (real_part, imag_part)


def columns_forward(values, outer_len, inner_len):
    extent = values[0].shape[0]
    shaped = tuple(
        (None if piece is None else piece.reshape(extent, outer_len, inner_len) for piece in values)
    )
    outer_idx = jnp.arange(outer_len)
    inner_idx = jnp.arange(inner_len)
    section = table_product(
        "ab,rbq->raq", rotation(outer_idx[:, None] * outer_idx[None, :], outer_len, -1.0), shaped
    )
    section = complex_mul(
        section, rotation(outer_idx[:, None] * inner_idx[None, :], outer_len * inner_len, -1.0)
    )
    return table_product(
        "bk,rpb->rpk", rotation(inner_idx[:, None] * inner_idx[None, :], inner_len, -1.0), section
    )


def columns_inverse(values, outer_len, inner_len, real_only):
    extent = values[0].shape[0]
    outer_idx = jnp.arange(outer_len)
    inner_idx = jnp.arange(inner_len)
    section = table_product(
        "bk,rpb->rpk", rotation(inner_idx[:, None] * inner_idx[None, :], inner_len, 1.0), values
    )
    section = complex_mul(
        section, rotation(outer_idx[:, None] * inner_idx[None, :], outer_len * inner_len, 1.0)
    )
    matrix = rotation(outer_idx[:, None] * outer_idx[None, :], outer_len, 1.0)
    if real_only:
        highest = lax.Precision.HIGHEST
        real_part = jnp.einsum("ab,rbq->raq", matrix[0], section[0], precision=highest)
        real_part = real_part - jnp.einsum("ab,rbq->raq", matrix[1], section[1], precision=highest)
        return real_part.reshape(extent, outer_len * inner_len)
    result = table_product("ab,rbq->raq", matrix, section)
    return (
        result[0].reshape(extent, outer_len * inner_len),
        result[1].reshape(extent, outer_len * inner_len),
    )


def rows_forward(values, freq_offset, full_width):
    extent = values[0].shape[0]
    positions = jnp.arange(extent)
    twiddle = rotation(positions * freq_offset, full_width, -1.0)
    values = complex_mul(values, (twiddle[0][:, None], twiddle[1][:, None]))
    return table_product(
        "sr,rc->sc", rotation(positions[:, None] * positions[None, :], extent, -1.0), values
    )


def rows_inverse(values, freq_offset, full_width):
    extent = values[0].shape[0]
    positions = jnp.arange(extent)
    values = table_product(
        "rs,sc->rc", rotation(positions[:, None] * positions[None, :], extent, 1.0), values
    )
    twiddle = rotation(positions * freq_offset, full_width, 1.0)
    return complex_mul(values, (twiddle[0][:, None], twiddle[1][:, None]))


def pairs_forward(stacked, num_bits):
    slab_index = lax.axis_index("slab")
    for bit_level in range(num_bits - 1, -1, -1):
        half_span = 2**bit_level
        partner = swapped(stacked, "slab", bit_level)
        is_upper = slab_index // half_span % 2 == 1
        twiddle = rotation(slab_index % half_span, 2 * half_span, -1.0)
        lower_val = stacked + partner
        difference = partner - stacked
        upper_val = jnp.stack(complex_mul((difference[0], difference[1]), twiddle))
        stacked = jnp.where(is_upper, upper_val, lower_val)
    return stacked


def pairs_inverse(stacked, num_bits):
    slab_index = lax.axis_index("slab")
    for bit_level in range(num_bits):
        half_span = 2**bit_level
        partner = swapped(stacked, "slab", bit_level)
        is_upper = slab_index // half_span % 2 == 1
        twiddle = rotation(slab_index % half_span, 2 * half_span, 1.0)
        from_upper = jnp.where(is_upper, stacked, partner)
        from_lower = jnp.where(is_upper, partner, stacked)
        turned = jnp.stack(complex_mul((from_upper[0], from_upper[1]), twiddle))
        stacked = jnp.where(is_upper, from_lower - turned, from_lower + turned)
    return stacked


def mix_forward(stacked, num_bits):
    return pairs_forward(stacked, num_bits)


def mix_inverse(stacked, num_bits):
    return pairs_inverse(stacked, num_bits)


def tap_band(kernel_taps, rows, cols, offset):
    diff = jnp.arange(rows)[:, None] - jnp.arange(cols)[None, :] - offset
    tap_idx = jnp.arange(kernel_taps.shape[0])[:, None, None]
    hits = jnp.where(diff[None] == tap_idx, kernel_taps[:, None, None], 0.0)
    return jnp.sum(hits, axis=0)


def blur_bands(kernel_taps, extent, block, margin):
    reach = (kernel_taps.shape[0] - 1) // 2
    row_band = tap_band(kernel_taps, extent + 2 * reach, extent, 0).T
    col_band = tap_band(kernel_taps, block + 2 * margin, block, margin - reach)
    return (row_band, col_band)


def smooth(padded, bands, extent, span):
    highest = lax.Precision.HIGHEST
    row_band, col_band = bands
    row_part = jnp.dot(row_band, padded, precision=highest)
    block = col_band.shape[1]
    margin = (col_band.shape[0] - block) // 2
    widened = jnp.pad(row_part, ((0, 0), (margin, margin)))
    windows = jnp.stack(
        [widened[:, j * block : j * block + block + 2 * margin] for j in range(span // block)], 1
    )
    result = jnp.einsum("rji,ib->rjb", windows, col_band, precision=highest)
    return result.reshape(extent, span)


def exchanged(shard, axis, offset):
    return lax.ppermute(shard, axis, [(i, i ^ offset) for i in range(lax.axis_size(axis))])


def digit_groups(count, radix):
    groups = []
    while count > 1:
        groups.append(min(radix, count))
        count //= min(radix, count)
    return groups


def reduce_scatter_cols(values, axis, radix=4):
    count = lax.axis_size(axis)
    index = lax.axis_index(axis)
    extent, width = values.shape
    groups = digit_groups(count, radix)
    values = values.reshape((extent,) + tuple(reversed(groups)) + (width // count,))
    stride = 1
    for level, size in enumerate(groups):
        dim = len(groups) - level
        mine = index // stride % size
        total = lax.dynamic_index_in_dim(values, mine, axis=dim, keepdims=False)
        for offset in range(1, size):
            send = lax.dynamic_index_in_dim(values, mine ^ offset, axis=dim, keepdims=False)
            total = total + exchanged(send, axis, offset * stride)
        values = total
        stride *= size
    return values.reshape(extent, width // count)


def all_gather_cols(values, axis, radix=4):
    count = lax.axis_size(axis)
    index = lax.axis_index(axis)
    extent, block = values.shape
    groups = digit_groups(count, radix)
    stride = count
    for size in reversed(groups):
        stride //= size
        mine = index // stride % size
        got = [values] + [exchanged(values, axis, offset * stride) for offset in range(1, size)]
        parts = []
        for slot in range(size):
            part = jnp.zeros_like(values)
            for offset in range(size):
                part = part + jnp.where((slot ^ mine) == offset, got[offset], 0.0)
            parts.append(part)
        values = jnp.stack(parts, values.ndim - 1)
    return values.reshape(extent, block * count)


def all_reduce_cols(values, axis, widen, radix=4):
    count = lax.axis_size(axis)
    index = lax.axis_index(axis)
    low = min(radix, count)
    high = count // low
    extent, width = values.shape
    values = values.reshape(extent, high, low, width // count)
    mine = index % low
    total = lax.dynamic_index_in_dim(values, mine, axis=2, keepdims=False)
    for offset in range(1, low):
        send = lax.dynamic_index_in_dim(values, mine ^ offset, axis=2, keepdims=False)
        total = total + exchanged(send, axis, offset)
    upper = index // low
    got = [total] + [exchanged(total, axis, offset * low) for offset in range(1, high)]
    summed = jnp.zeros_like(total)
    for slot in range(high):
        term = jnp.zeros_like(total)
        for offset in range(high):
            term = term + jnp.where((slot ^ upper) == offset, got[offset], 0.0)
        summed = summed + term
    summed = widen(summed)
    got = [summed] + [exchanged(summed, axis, offset) for offset in range(1, low)]
    parts = []
    for slot in range(low):
        part = jnp.zeros_like(summed)
        for offset in range(low):
            part = part + jnp.where((slot ^ mine) == offset, got[offset], 0.0)
        parts.append(part)
    return jnp.stack(parts, 2).reshape(summed.shape[0], width)


def resist_section(intensity_term, kernel_taps, target, kern_count, kern_index):
    reach = (kernel_taps.shape[0] - 1) // 2
    flipped = kernel_taps[::-1]
    extent, full_width = intensity_term.shape
    share_cols = full_width // kern_count
    wide = extent + 2 * reach
    bands = lax.optimization_barrier(
        (blur_bands(kernel_taps, wide, 128, 64), blur_bands(flipped, extent, 128, 64))
    )
    goal_cells = padded_2(target, (("slab", 0),), reach).astype(jnp.float32)
    summed = all_reduce_cols(
        intensity_term, "kern", lambda block: padded_2(block, (("slab", 0),), 2 * reach)
    )
    resist = jax.nn.sigmoid(STEEP * (smooth(summed, bands[0], wide, full_width) - LEVEL))
    first_row = lax.axis_index("slab") * extent - reach
    rows = first_row + jnp.arange(wide)
    inside = (rows >= 0) & (rows < lax.axis_size("slab") * extent)
    slope_grad = 2.0 * (resist - goal_cells) * STEEP * resist * (1.0 - resist)
    slope_grad = jnp.where(inside[:, None], slope_grad, 0.0)
    cotangent = smooth(slope_grad, bands[1], extent, full_width)
    resist = lax.dynamic_slice_in_dim(resist[reach : reach + extent], kern_index * share_cols, share_cols, 1)
    return (cotangent, resist)


def to_columns(stacked):
    pieces, extent, width = stacked.shape
    count = lax.axis_size("slab")
    share = width // count
    split = stacked.reshape(pieces, extent, count, share).transpose(2, 0, 1, 3)
    split = split.reshape(count, pieces * extent * share // 128, 128)
    joined = lax.all_to_all(split, "slab", 0, 0, tiled=True)
    return joined.reshape(count, pieces, extent, share).transpose(1, 0, 2, 3)


def to_rows(stacked):
    pieces, count, extent, share = stacked.shape
    split = stacked.transpose(1, 0, 2, 3).reshape(count, pieces * extent * share // 128, 128)
    joined = lax.all_to_all(split, "slab", 0, 0, tiled=True).reshape(count, pieces, extent, share)
    return joined.transpose(1, 2, 0, 3).reshape(pieces, extent, count * share)


def row_tables(count, extent, sign_val):
    num_bits = count.bit_length() - 1
    slab_idx = jnp.arange(count)
    local_idx = jnp.arange(extent)
    flipped = reversed_bits(slab_idx, num_bits)
    across = rotation(flipped[:, None] * slab_idx[None, :], count, sign_val)
    twiddle = rotation(flipped[:, None] * local_idx[None, :], count * extent, sign_val)
    within = rotation(local_idx[:, None] * local_idx[None, :], extent, sign_val)
    return (across, twiddle, within)


def rows_forward_t(values):
    count, extent, _ = values[0].shape
    across, twiddle, within = row_tables(count, extent, -1.0)
    values = table_product("ed,dpv->epv", across, values)
    values = complex_mul(values, (twiddle[0][:, :, None], twiddle[1][:, :, None]))
    return table_product("qp,epv->eqv", within, values)


def rows_inverse_t(values):
    count, extent, _ = values[0].shape
    across, twiddle, within = row_tables(count, extent, 1.0)
    values = table_product("pq,eqv->epv", within, values)
    values = complex_mul(values, (twiddle[0][:, :, None], twiddle[1][:, :, None]))
    return table_product("ed,epv->dpv", across, values)


def on_device(mask_level, kernel_spectra, socs_weight, kernel_slot, blur_taps, target):
    extent, full_width = mask_level.shape
    slab_count = lax.axis_size("slab")
    kern_count = lax.axis_size("kern")
    num_bits = slab_count.bit_length() - 1
    inner_len = CQ
    outer_len = full_width // inner_len
    freq_offset = reversed_bits(lax.axis_index("slab"), num_bits)
    kern_index = lax.axis_index("kern")
    kernel_id = jnp.sum(jnp.where(jnp.arange(kernel_slot.shape[0]) == kern_index, kernel_slot, 0))
    weight = jnp.sum(jnp.where(jnp.arange(socs_weight.shape[0]) == kernel_id, socs_weight, 0.0))
    arranged = kernel_spectra[0].reshape(2, extent, inner_len, outer_len).transpose(0, 1, 3, 2)
    arranged = to_columns(arranged.reshape(2, extent, full_width))
    transfer = (arranged[0], arranged[1])
    norm_scale = 1.0 / (full_width * full_width)

    def spectrum(values):
        columns = columns_forward(values, outer_len, inner_len)
        stacked = to_columns(jnp.stack(columns).reshape(2, extent, full_width))
        return rows_forward_t((stacked[0], stacked[1]))

    def back_to_cells(spectral, real_only):
        stacked = to_rows(jnp.stack(rows_inverse_t(spectral)))
        shaped = (
            stacked[0].reshape(extent, outer_len, inner_len),
            stacked[1].reshape(extent, outer_len, inner_len),
        )
        return columns_inverse(shaped, outer_len, inner_len, real_only)

    mask_spec = spectrum((mask_level, None))
    field_val = back_to_cells(complex_mul(transfer, mask_spec), False)
    field_val = (field_val[0] * norm_scale, field_val[1] * norm_scale)
    intensity_term = weight * (field_val[0] * field_val[0] + field_val[1] * field_val[1])
    cotangent, resist = resist_section(intensity_term, blur_taps, target, kern_count, kern_index)
    factor = 2.0 * weight * cotangent
    carried_spec = spectrum((factor * field_val[0], factor * field_val[1]))
    gradient_term = (
        back_to_cells(complex_mul((transfer[0], -transfer[1]), carried_spec), True) * norm_scale
    )
    gradient = reduce_scatter_cols(gradient_term, "kern")
    return (gradient, resist)


def solution(mesh):
    placed = (P("slab", None), P("kern", None, "slab", None), P(), P(), P(), P("slab", None))
    return jax.shard_map(
        on_device,
        mesh=mesh,
        in_specs=placed,
        out_specs=(P("slab", "kern"), P("slab", "kern")),
        check_vma=False,
    )
```

```python
import math

import jax
import jax.numpy as jnp
from jax import lax
from jax.sharding import PartitionSpec as P

CQ = 128


STEEP = 4.0
LEVEL = 0.5


def swapped(shard, axis, apart):
    return lax.ppermute(shard, axis, [(i, i ^ 1 << apart) for i in range(lax.axis_size(axis))])


def padded_2(shard, sides, width):
    for axis, dim in sides:
        devices, length = (lax.axis_size(axis), shard.shape[dim])
        up = [(i, (i + 1) % devices) for i in range(devices - 1)]
        down = [(j, i) for i, j in up]
        last = lax.slice_in_dim(shard, length - width, length, axis=dim)
        initial = lax.slice_in_dim(shard, 0, width, axis=dim)
        before = lax.ppermute(last, axis, up)
        after = lax.ppermute(initial, axis, down)
        shard = jnp.concatenate([before, shard, after], axis=dim)
    return shard


def reversed_bits(number, num_bits):
    result = number * 0
    for bit_pos in range(num_bits):
        result = result * 2 + number // 2**bit_pos % 2
    return result


def rotation(product, length, sign_val):
    fraction = (product % length).astype(jnp.float32) / length
    angles = sign_val * 2.0 * math.pi * fraction
    return (jnp.cos(angles), jnp.sin(angles))


def complex_mul(first_pair, second_pair):
    real_part = first_pair[0] * second_pair[0] - first_pair[1] * second_pair[1]
    imag_part = first_pair[0] * second_pair[1] + first_pair[1] * second_pair[0]
    return (real_part, imag_part)


def table_product(pattern, matrix, values):
    highest = lax.Precision.HIGHEST

    def single(first_op, second_op):
        return jnp.einsum(pattern, first_op, second_op, precision=highest)

    if values[1] is None:
        return (single(matrix[0], values[0]), single(matrix[1], values[0]))
    real_part = single(matrix[0], values[0]) - single(matrix[1], values[1])
    imag_part = single(matrix[0], values[1]) + single(matrix[1], values[0])
    return (real_part, imag_part)


def columns_forward(values, outer_len, inner_len):
    extent = values[0].shape[0]
    shaped = tuple(
        (None if piece is None else piece.reshape(extent, outer_len, inner_len) for piece in values)
    )
    outer_idx = jnp.arange(outer_len)
    inner_idx = jnp.arange(inner_len)
    section = table_product(
        "ab,rbq->raq", rotation(outer_idx[:, None] * outer_idx[None, :], outer_len, -1.0), shaped
    )
    section = complex_mul(
        section, rotation(outer_idx[:, None] * inner_idx[None, :], outer_len * inner_len, -1.0)
    )
    return table_product(
        "bk,rpb->rpk", rotation(inner_idx[:, None] * inner_idx[None, :], inner_len, -1.0), section
    )


def columns_inverse(values, outer_len, inner_len, real_only):
    extent = values[0].shape[0]
    outer_idx = jnp.arange(outer_len)
    inner_idx = jnp.arange(inner_len)
    section = table_product(
        "bk,rpb->rpk", rotation(inner_idx[:, None] * inner_idx[None, :], inner_len, 1.0), values
    )
    section = complex_mul(
        section, rotation(outer_idx[:, None] * inner_idx[None, :], outer_len * inner_len, 1.0)
    )
    matrix = rotation(outer_idx[:, None] * outer_idx[None, :], outer_len, 1.0)
    if real_only:
        highest = lax.Precision.HIGHEST
        real_part = jnp.einsum("ab,rbq->raq", matrix[0], section[0], precision=highest)
        real_part = real_part - jnp.einsum("ab,rbq->raq", matrix[1], section[1], precision=highest)
        return real_part.reshape(extent, outer_len * inner_len)
    result = table_product("ab,rbq->raq", matrix, section)
    return (
        result[0].reshape(extent, outer_len * inner_len),
        result[1].reshape(extent, outer_len * inner_len),
    )


def rows_forward(values, freq_offset, full_width):
    extent = values[0].shape[0]
    positions = jnp.arange(extent)
    twiddle = rotation(positions * freq_offset, full_width, -1.0)
    values = complex_mul(values, (twiddle[0][:, None], twiddle[1][:, None]))
    return table_product(
        "sr,rc->sc", rotation(positions[:, None] * positions[None, :], extent, -1.0), values
    )


def rows_inverse(values, freq_offset, full_width):
    extent = values[0].shape[0]
    positions = jnp.arange(extent)
    values = table_product(
        "rs,sc->rc", rotation(positions[:, None] * positions[None, :], extent, 1.0), values
    )
    twiddle = rotation(positions * freq_offset, full_width, 1.0)
    return complex_mul(values, (twiddle[0][:, None], twiddle[1][:, None]))


def pairs_forward(stacked, num_bits):
    slab_index = lax.axis_index("slab")
    for bit_level in range(num_bits - 1, -1, -1):
        half_span = 2**bit_level
        partner = swapped(stacked, "slab", bit_level)
        is_upper = slab_index // half_span % 2 == 1
        twiddle = rotation(slab_index % half_span, 2 * half_span, -1.0)
        lower_val = stacked + partner
        difference = partner - stacked
        upper_val = jnp.stack(complex_mul((difference[0], difference[1]), twiddle))
        stacked = jnp.where(is_upper, upper_val, lower_val)
    return stacked


def pairs_inverse(stacked, num_bits):
    slab_index = lax.axis_index("slab")
    for bit_level in range(num_bits):
        half_span = 2**bit_level
        partner = swapped(stacked, "slab", bit_level)
        is_upper = slab_index // half_span % 2 == 1
        twiddle = rotation(slab_index % half_span, 2 * half_span, 1.0)
        from_upper = jnp.where(is_upper, stacked, partner)
        from_lower = jnp.where(is_upper, partner, stacked)
        turned = jnp.stack(complex_mul((from_upper[0], from_upper[1]), twiddle))
        stacked = jnp.where(is_upper, from_lower - turned, from_lower + turned)
    return stacked


def mix_forward(stacked, num_bits):
    return pairs_forward(stacked, num_bits)


def mix_inverse(stacked, num_bits):
    return pairs_inverse(stacked, num_bits)


def tap_band(kernel_taps, rows, cols, offset):
    diff = jnp.arange(rows)[:, None] - jnp.arange(cols)[None, :] - offset
    tap_idx = jnp.arange(kernel_taps.shape[0])[:, None, None]
    hits = jnp.where(diff[None] == tap_idx, kernel_taps[:, None, None], 0.0)
    return jnp.sum(hits, axis=0)


def blur_bands(kernel_taps, extent, block, margin):
    reach = (kernel_taps.shape[0] - 1) // 2
    row_band = tap_band(kernel_taps, extent + 2 * reach, extent, 0).T
    col_band = tap_band(kernel_taps, block + 2 * margin, block, margin - reach)
    return (row_band, col_band)


def smooth(padded, bands, extent, span):
    highest = lax.Precision.HIGHEST
    row_band, col_band = bands
    row_part = jnp.dot(row_band, padded, precision=highest)
    block = col_band.shape[1]
    margin = (col_band.shape[0] - block) // 2
    widened = jnp.pad(row_part, ((0, 0), (margin, margin)))
    windows = jnp.stack(
        [widened[:, j * block : j * block + block + 2 * margin] for j in range(span // block)], 1
    )
    result = jnp.einsum("rji,ib->rjb", windows, col_band, precision=highest)
    return result.reshape(extent, span)


def exchanged(shard, axis, offset):
    return lax.ppermute(shard, axis, [(i, i ^ offset) for i in range(lax.axis_size(axis))])


def digit_groups(count, radix):
    groups = []
    while count > 1:
        groups.append(min(radix, count))
        count //= min(radix, count)
    return groups


def reduce_scatter_cols(values, axis, radix=4):
    count = lax.axis_size(axis)
    index = lax.axis_index(axis)
    extent, width = values.shape
    groups = digit_groups(count, radix)
    values = values.reshape((extent,) + tuple(reversed(groups)) + (width // count,))
    stride = 1
    for level, size in enumerate(groups):
        dim = len(groups) - level
        mine = index // stride % size
        total = lax.dynamic_index_in_dim(values, mine, axis=dim, keepdims=False)
        for offset in range(1, size):
            send = lax.dynamic_index_in_dim(values, mine ^ offset, axis=dim, keepdims=False)
            total = total + exchanged(send, axis, offset * stride)
        values = total
        stride *= size
    return values.reshape(extent, width // count)


def all_gather_cols(values, axis, radix=4):
    count = lax.axis_size(axis)
    index = lax.axis_index(axis)
    extent, block = values.shape
    groups = digit_groups(count, radix)
    stride = count
    for size in reversed(groups):
        stride //= size
        mine = index // stride % size
        got = [values] + [exchanged(values, axis, offset * stride) for offset in range(1, size)]
        parts = []
        for slot in range(size):
            part = jnp.zeros_like(values)
            for offset in range(size):
                part = part + jnp.where((slot ^ mine) == offset, got[offset], 0.0)
            parts.append(part)
        values = jnp.stack(parts, values.ndim - 1)
    return values.reshape(extent, block * count)


def all_reduce_cols(values, axis, widen, radix=4):
    count = lax.axis_size(axis)
    index = lax.axis_index(axis)
    low = min(radix, count)
    high = count // low
    extent, width = values.shape
    values = values.reshape(extent, high, low, width // count)
    mine = index % low
    total = lax.dynamic_index_in_dim(values, mine, axis=2, keepdims=False)
    for offset in range(1, low):
        send = lax.dynamic_index_in_dim(values, mine ^ offset, axis=2, keepdims=False)
        total = total + exchanged(send, axis, offset)
    upper = index // low
    got = [total] + [exchanged(total, axis, offset * low) for offset in range(1, high)]
    summed = jnp.zeros_like(total)
    for slot in range(high):
        term = jnp.zeros_like(total)
        for offset in range(high):
            term = term + jnp.where((slot ^ upper) == offset, got[offset], 0.0)
        summed = summed + term
    summed = widen(summed)
    got = [summed] + [exchanged(summed, axis, offset) for offset in range(1, low)]
    parts = []
    for slot in range(low):
        part = jnp.zeros_like(summed)
        for offset in range(low):
            part = part + jnp.where((slot ^ mine) == offset, got[offset], 0.0)
        parts.append(part)
    return jnp.stack(parts, 2).reshape(summed.shape[0], width)


def resist_section(intensity_term, kernel_taps, target, kern_count, kern_index):
    reach = (kernel_taps.shape[0] - 1) // 2
    flipped = kernel_taps[::-1]
    extent, full_width = intensity_term.shape
    share_cols = full_width // kern_count
    wide = extent + 2 * reach
    bands = lax.optimization_barrier(
        (blur_bands(kernel_taps, wide, 128, 64), blur_bands(flipped, extent, 128, 64))
    )
    goal_cells = padded_2(target, (("slab", 0),), reach).astype(jnp.float32)
    summed = all_reduce_cols(
        intensity_term, "kern", lambda block: padded_2(block, (("slab", 0),), 2 * reach)
    )
    resist = jax.nn.sigmoid(STEEP * (smooth(summed, bands[0], wide, full_width) - LEVEL))
    first_row = lax.axis_index("slab") * extent - reach
    rows = first_row + jnp.arange(wide)
    inside = (rows >= 0) & (rows < lax.axis_size("slab") * extent)
    slope_grad = 2.0 * (resist - goal_cells) * STEEP * resist * (1.0 - resist)
    slope_grad = jnp.where(inside[:, None], slope_grad, 0.0)
    cotangent = smooth(slope_grad, bands[1], extent, full_width)
    resist = lax.dynamic_slice_in_dim(resist[reach : reach + extent], kern_index * share_cols, share_cols, 1)
    return (cotangent, resist)


def to_columns(stacked):
    pieces, extent, width = stacked.shape
    count = lax.axis_size("slab")
    share = width // count
    split = stacked.reshape(pieces, extent, count, share).transpose(2, 0, 1, 3)
    split = split.reshape(count, pieces * extent * share // 128, 128)
    joined = lax.all_to_all(split, "slab", 0, 0, tiled=True)
    return joined.reshape(count, pieces, extent, share).transpose(1, 0, 2, 3)


def to_rows(stacked):
    pieces, count, extent, share = stacked.shape
    split = stacked.transpose(1, 0, 2, 3).reshape(count, pieces * extent * share // 128, 128)
    joined = lax.all_to_all(split, "slab", 0, 0, tiled=True).reshape(count, pieces, extent, share)
    return joined.transpose(1, 2, 0, 3).reshape(pieces, extent, count * share)


def row_tables(count, extent, sign_val):
    num_bits = count.bit_length() - 1
    slab_idx = jnp.arange(count)
    local_idx = jnp.arange(extent)
    flipped = reversed_bits(slab_idx, num_bits)
    across = rotation(flipped[:, None] * slab_idx[None, :], count, sign_val)
    twiddle = rotation(flipped[:, None] * local_idx[None, :], count * extent, sign_val)
    within = rotation(local_idx[:, None] * local_idx[None, :], extent, sign_val)
    return (across, twiddle, within)


def rows_forward_t(values):
    count, extent, _ = values[0].shape
    across, twiddle, within = row_tables(count, extent, -1.0)
    values = table_product("ed,dpv->epv", across, values)
    values = complex_mul(values, (twiddle[0][:, :, None], twiddle[1][:, :, None]))
    return table_product("qp,epv->eqv", within, values)


def rows_inverse_t(values):
    count, extent, _ = values[0].shape
    across, twiddle, within = row_tables(count, extent, 1.0)
    values = table_product("pq,eqv->epv", within, values)
    values = complex_mul(values, (twiddle[0][:, :, None], twiddle[1][:, :, None]))
    return table_product("ed,epv->dpv", across, values)


def on_device(mask_level, kernel_spectra, socs_weight, kernel_slot, blur_taps, target):
    extent, full_width = mask_level.shape
    slab_count = lax.axis_size("slab")
    kern_count = lax.axis_size("kern")
    num_bits = slab_count.bit_length() - 1
    inner_len = CQ
    outer_len = full_width // inner_len
    freq_offset = reversed_bits(lax.axis_index("slab"), num_bits)
    kern_index = lax.axis_index("kern")
    kernel_id = jnp.sum(jnp.where(jnp.arange(kernel_slot.shape[0]) == kern_index, kernel_slot, 0))
    weight = jnp.sum(jnp.where(jnp.arange(socs_weight.shape[0]) == kernel_id, socs_weight, 0.0))
    arranged = kernel_spectra[0].reshape(2, extent, inner_len, outer_len).transpose(0, 1, 3, 2)
    norm_scale = 1.0 / (full_width * full_width)

    def spectrum(values):
        columns = columns_forward(values, outer_len, inner_len)
        stacked = to_columns(jnp.stack(columns).reshape(2, extent, full_width))
        return (stacked, rows_forward_t((stacked[0], stacked[1])))

    def back_to_cells(spectral, real_only):
        stacked = to_rows(jnp.stack(rows_inverse_t(spectral)))
        shaped = (
            stacked[0].reshape(extent, outer_len, inner_len),
            stacked[1].reshape(extent, outer_len, inner_len),
        )
        return columns_inverse(shaped, outer_len, inner_len, real_only)

    mask_cols, mask_spec = spectrum((mask_level, None))
    arranged = lax.optimization_barrier((mask_cols, arranged))[1]
    arranged = to_columns(arranged.reshape(2, extent, full_width))
    transfer = (arranged[0], arranged[1])
    field_val = back_to_cells(complex_mul(transfer, mask_spec), False)
    field_val = (field_val[0] * norm_scale, field_val[1] * norm_scale)
    intensity_term = weight * (field_val[0] * field_val[0] + field_val[1] * field_val[1])
    cotangent, resist = resist_section(intensity_term, blur_taps, target, kern_count, kern_index)
    factor = 2.0 * weight * cotangent
    carried_spec = spectrum((factor * field_val[0], factor * field_val[1]))[1]
    gradient_term = (
        back_to_cells(complex_mul((transfer[0], -transfer[1]), carried_spec), True) * norm_scale
    )
    gradient = reduce_scatter_cols(gradient_term, "kern")
    return (gradient, resist)


def solution(mesh):
    placed = (P("slab", None), P("kern", None, "slab", None), P(), P(), P(), P("slab", None))
    return jax.shard_map(
        on_device,
        mesh=mesh,
        in_specs=placed,
        out_specs=(P("slab", "kern"), P("slab", "kern")),
        check_vma=False,
    )
```

```python
import math

import jax
import jax.numpy as jnp
from jax import lax
from jax.sharding import PartitionSpec as P

CQ = 128


STEEP = 4.0
LEVEL = 0.5


def swapped(shard, axis, apart):
    return lax.ppermute(shard, axis, [(i, i ^ 1 << apart) for i in range(lax.axis_size(axis))])


def padded_2(shard, sides, width):
    for axis, dim in sides:
        devices, length = (lax.axis_size(axis), shard.shape[dim])
        up = [(i, (i + 1) % devices) for i in range(devices - 1)]
        down = [(j, i) for i, j in up]
        last = lax.slice_in_dim(shard, length - width, length, axis=dim)
        initial = lax.slice_in_dim(shard, 0, width, axis=dim)
        before = lax.ppermute(last, axis, up)
        after = lax.ppermute(initial, axis, down)
        shard = jnp.concatenate([before, shard, after], axis=dim)
    return shard


def reversed_bits(number, num_bits):
    result = number * 0
    for bit_pos in range(num_bits):
        result = result * 2 + number // 2**bit_pos % 2
    return result


def rotation(product, length, sign_val):
    fraction = (product % length).astype(jnp.float32) / length
    angles = sign_val * 2.0 * math.pi * fraction
    return (jnp.cos(angles), jnp.sin(angles))


def complex_mul(first_pair, second_pair):
    real_part = first_pair[0] * second_pair[0] - first_pair[1] * second_pair[1]
    imag_part = first_pair[0] * second_pair[1] + first_pair[1] * second_pair[0]
    return (real_part, imag_part)


def table_product(pattern, matrix, values):
    highest = lax.Precision.HIGHEST

    def single(first_op, second_op):
        return jnp.einsum(pattern, first_op, second_op, precision=highest)

    if values[1] is None:
        return (single(matrix[0], values[0]), single(matrix[1], values[0]))
    real_part = single(matrix[0], values[0]) - single(matrix[1], values[1])
    imag_part = single(matrix[0], values[1]) + single(matrix[1], values[0])
    return (real_part, imag_part)


def columns_forward(values, outer_len, inner_len):
    extent = values[0].shape[0]
    shaped = tuple(
        (None if piece is None else piece.reshape(extent, outer_len, inner_len) for piece in values)
    )
    outer_idx = jnp.arange(outer_len)
    inner_idx = jnp.arange(inner_len)
    section = table_product(
        "ab,rbq->raq", rotation(outer_idx[:, None] * outer_idx[None, :], outer_len, -1.0), shaped
    )
    section = complex_mul(
        section, rotation(outer_idx[:, None] * inner_idx[None, :], outer_len * inner_len, -1.0)
    )
    return table_product(
        "bk,rpb->rpk", rotation(inner_idx[:, None] * inner_idx[None, :], inner_len, -1.0), section
    )


def columns_inverse(values, outer_len, inner_len, real_only):
    extent = values[0].shape[0]
    outer_idx = jnp.arange(outer_len)
    inner_idx = jnp.arange(inner_len)
    section = table_product(
        "bk,rpb->rpk", rotation(inner_idx[:, None] * inner_idx[None, :], inner_len, 1.0), values
    )
    section = complex_mul(
        section, rotation(outer_idx[:, None] * inner_idx[None, :], outer_len * inner_len, 1.0)
    )
    matrix = rotation(outer_idx[:, None] * outer_idx[None, :], outer_len, 1.0)
    if real_only:
        highest = lax.Precision.HIGHEST
        real_part = jnp.einsum("ab,rbq->raq", matrix[0], section[0], precision=highest)
        real_part = real_part - jnp.einsum("ab,rbq->raq", matrix[1], section[1], precision=highest)
        return real_part.reshape(extent, outer_len * inner_len)
    result = table_product("ab,rbq->raq", matrix, section)
    return (
        result[0].reshape(extent, outer_len * inner_len),
        result[1].reshape(extent, outer_len * inner_len),
    )


def rows_forward(values, freq_offset, full_width):
    extent = values[0].shape[0]
    positions = jnp.arange(extent)
    twiddle = rotation(positions * freq_offset, full_width, -1.0)
    values = complex_mul(values, (twiddle[0][:, None], twiddle[1][:, None]))
    return table_product(
        "sr,rc->sc", rotation(positions[:, None] * positions[None, :], extent, -1.0), values
    )


def rows_inverse(values, freq_offset, full_width):
    extent = values[0].shape[0]
    positions = jnp.arange(extent)
    values = table_product(
        "rs,sc->rc", rotation(positions[:, None] * positions[None, :], extent, 1.0), values
    )
    twiddle = rotation(positions * freq_offset, full_width, 1.0)
    return complex_mul(values, (twiddle[0][:, None], twiddle[1][:, None]))


def pairs_forward(stacked, num_bits):
    slab_index = lax.axis_index("slab")
    for bit_level in range(num_bits - 1, -1, -1):
        half_span = 2**bit_level
        partner = swapped(stacked, "slab", bit_level)
        is_upper = slab_index // half_span % 2 == 1
        twiddle = rotation(slab_index % half_span, 2 * half_span, -1.0)
        lower_val = stacked + partner
        difference = partner - stacked
        upper_val = jnp.stack(complex_mul((difference[0], difference[1]), twiddle))
        stacked = jnp.where(is_upper, upper_val, lower_val)
    return stacked


def pairs_inverse(stacked, num_bits):
    slab_index = lax.axis_index("slab")
    for bit_level in range(num_bits):
        half_span = 2**bit_level
        partner = swapped(stacked, "slab", bit_level)
        is_upper = slab_index // half_span % 2 == 1
        twiddle = rotation(slab_index % half_span, 2 * half_span, 1.0)
        from_upper = jnp.where(is_upper, stacked, partner)
        from_lower = jnp.where(is_upper, partner, stacked)
        turned = jnp.stack(complex_mul((from_upper[0], from_upper[1]), twiddle))
        stacked = jnp.where(is_upper, from_lower - turned, from_lower + turned)
    return stacked


def mix_forward(stacked, num_bits):
    return pairs_forward(stacked, num_bits)


def mix_inverse(stacked, num_bits):
    return pairs_inverse(stacked, num_bits)


def tap_band(kernel_taps, rows, cols, offset):
    diff = jnp.arange(rows)[:, None] - jnp.arange(cols)[None, :] - offset
    tap_idx = jnp.arange(kernel_taps.shape[0])[:, None, None]
    hits = jnp.where(diff[None] == tap_idx, kernel_taps[:, None, None], 0.0)
    return jnp.sum(hits, axis=0)


def blur_bands(kernel_taps, extent, block, margin):
    reach = (kernel_taps.shape[0] - 1) // 2
    row_band = tap_band(kernel_taps, extent + 2 * reach, extent, 0).T
    col_band = tap_band(kernel_taps, block + 2 * margin, block, margin - reach)
    return (row_band, col_band)


def smooth(padded, bands, extent, span):
    highest = lax.Precision.HIGHEST
    row_band, col_band = bands
    row_part = jnp.dot(row_band, padded, precision=highest)
    block = col_band.shape[1]
    margin = (col_band.shape[0] - block) // 2
    widened = jnp.pad(row_part, ((0, 0), (margin, margin)))
    windows = jnp.stack(
        [widened[:, j * block : j * block + block + 2 * margin] for j in range(span // block)], 1
    )
    result = jnp.einsum("rji,ib->rjb", windows, col_band, precision=highest)
    return result.reshape(extent, span)


def exchanged(shard, axis, offset):
    return lax.ppermute(shard, axis, [(i, i ^ offset) for i in range(lax.axis_size(axis))])


def digit_groups(count, radix):
    groups = []
    while count > 1:
        groups.append(min(radix, count))
        count //= min(radix, count)
    return groups


def reduce_scatter_cols(values, axis, radix=4):
    count = lax.axis_size(axis)
    index = lax.axis_index(axis)
    extent, width = values.shape
    groups = digit_groups(count, radix)
    values = values.reshape((extent,) + tuple(reversed(groups)) + (width // count,))
    stride = 1
    for level, size in enumerate(groups):
        dim = len(groups) - level
        mine = index // stride % size
        total = lax.dynamic_index_in_dim(values, mine, axis=dim, keepdims=False)
        for offset in range(1, size):
            send = lax.dynamic_index_in_dim(values, mine ^ offset, axis=dim, keepdims=False)
            total = total + exchanged(send, axis, offset * stride)
        values = total
        stride *= size
    return values.reshape(extent, width // count)


def all_gather_cols(values, axis, radix=4):
    count = lax.axis_size(axis)
    index = lax.axis_index(axis)
    extent, block = values.shape
    groups = digit_groups(count, radix)
    stride = count
    for size in reversed(groups):
        stride //= size
        mine = index // stride % size
        got = [values] + [exchanged(values, axis, offset * stride) for offset in range(1, size)]
        parts = []
        for slot in range(size):
            part = jnp.zeros_like(values)
            for offset in range(size):
                part = part + jnp.where((slot ^ mine) == offset, got[offset], 0.0)
            parts.append(part)
        values = jnp.stack(parts, values.ndim - 1)
    return values.reshape(extent, block * count)


def scatter_sum_cols(values, axis):
    count = lax.axis_size(axis)
    extent, width = values.shape
    share = width // count
    split = values.reshape(extent, count, share).transpose(1, 0, 2)
    split = split.reshape(count, extent * share // 128, 128)
    joined = lax.all_to_all(split, axis, 0, 0, tiled=True)
    return jnp.sum(joined, axis=0).reshape(extent, share)


def all_reduce_cols(values, axis, widen, radix=4):
    count = lax.axis_size(axis)
    index = lax.axis_index(axis)
    low = min(radix, count)
    high = count // low
    extent, width = values.shape
    values = values.reshape(extent, high, low, width // count)
    mine = index % low
    total = lax.dynamic_index_in_dim(values, mine, axis=2, keepdims=False)
    for offset in range(1, low):
        send = lax.dynamic_index_in_dim(values, mine ^ offset, axis=2, keepdims=False)
        total = total + exchanged(send, axis, offset)
    upper = index // low
    got = [total] + [exchanged(total, axis, offset * low) for offset in range(1, high)]
    summed = jnp.zeros_like(total)
    for slot in range(high):
        term = jnp.zeros_like(total)
        for offset in range(high):
            term = term + jnp.where((slot ^ upper) == offset, got[offset], 0.0)
        summed = summed + term
    summed = widen(summed)
    got = [summed] + [exchanged(summed, axis, offset) for offset in range(1, low)]
    parts = []
    for slot in range(low):
        part = jnp.zeros_like(summed)
        for offset in range(low):
            part = part + jnp.where((slot ^ mine) == offset, got[offset], 0.0)
        parts.append(part)
    return jnp.stack(parts, 2).reshape(summed.shape[0], width)


def resist_section(intensity_term, kernel_taps, target, kern_count, kern_index):
    reach = (kernel_taps.shape[0] - 1) // 2
    flipped = kernel_taps[::-1]
    extent, full_width = intensity_term.shape
    share_cols = full_width // kern_count
    wide = extent + 2 * reach
    bands = lax.optimization_barrier(
        (blur_bands(kernel_taps, wide, 128, 64), blur_bands(flipped, extent, 128, 64))
    )
    goal_cells = padded_2(target, (("slab", 0),), reach).astype(jnp.float32)
    summed = all_reduce_cols(
        intensity_term, "kern", lambda block: padded_2(block, (("slab", 0),), 2 * reach)
    )
    resist = jax.nn.sigmoid(STEEP * (smooth(summed, bands[0], wide, full_width) - LEVEL))
    first_row = lax.axis_index("slab") * extent - reach
    rows = first_row + jnp.arange(wide)
    inside = (rows >= 0) & (rows < lax.axis_size("slab") * extent)
    slope_grad = 2.0 * (resist - goal_cells) * STEEP * resist * (1.0 - resist)
    slope_grad = jnp.where(inside[:, None], slope_grad, 0.0)
    cotangent = smooth(slope_grad, bands[1], extent, full_width)
    resist = lax.dynamic_slice_in_dim(resist[reach : reach + extent], kern_index * share_cols, share_cols, 1)
    return (cotangent, resist)


def to_columns(stacked):
    pieces, extent, width = stacked.shape
    count = lax.axis_size("slab")
    share = width // count
    split = stacked.reshape(pieces, extent, count, share).transpose(2, 0, 1, 3)
    split = split.reshape(count, pieces * extent * share // 128, 128)
    joined = lax.all_to_all(split, "slab", 0, 0, tiled=True)
    return joined.reshape(count, pieces, extent, share).transpose(1, 0, 2, 3)


def to_rows(stacked):
    pieces, count, extent, share = stacked.shape
    split = stacked.transpose(1, 0, 2, 3).reshape(count, pieces * extent * share // 128, 128)
    joined = lax.all_to_all(split, "slab", 0, 0, tiled=True).reshape(count, pieces, extent, share)
    return joined.transpose(1, 2, 0, 3).reshape(pieces, extent, count * share)


def row_tables(count, extent, sign_val):
    num_bits = count.bit_length() - 1
    slab_idx = jnp.arange(count)
    local_idx = jnp.arange(extent)
    flipped = reversed_bits(slab_idx, num_bits)
    across = rotation(flipped[:, None] * slab_idx[None, :], count, sign_val)
    twiddle = rotation(flipped[:, None] * local_idx[None, :], count * extent, sign_val)
    within = rotation(local_idx[:, None] * local_idx[None, :], extent, sign_val)
    return (across, twiddle, within)


def rows_forward_t(values):
    count, extent, _ = values[0].shape
    across, twiddle, within = row_tables(count, extent, -1.0)
    values = table_product("ed,dpv->epv", across, values)
    values = complex_mul(values, (twiddle[0][:, :, None], twiddle[1][:, :, None]))
    return table_product("qp,epv->eqv", within, values)


def rows_inverse_t(values):
    count, extent, _ = values[0].shape
    across, twiddle, within = row_tables(count, extent, 1.0)
    values = table_product("pq,eqv->epv", within, values)
    values = complex_mul(values, (twiddle[0][:, :, None], twiddle[1][:, :, None]))
    return table_product("ed,epv->dpv", across, values)


def on_device(mask_level, kernel_spectra, socs_weight, kernel_slot, blur_taps, target):
    extent, full_width = mask_level.shape
    slab_count = lax.axis_size("slab")
    kern_count = lax.axis_size("kern")
    num_bits = slab_count.bit_length() - 1
    inner_len = CQ
    outer_len = full_width // inner_len
    freq_offset = reversed_bits(lax.axis_index("slab"), num_bits)
    kern_index = lax.axis_index("kern")
    kernel_id = jnp.sum(jnp.where(jnp.arange(kernel_slot.shape[0]) == kern_index, kernel_slot, 0))
    weight = jnp.sum(jnp.where(jnp.arange(socs_weight.shape[0]) == kernel_id, socs_weight, 0.0))
    arranged = kernel_spectra[0].reshape(2, extent, inner_len, outer_len).transpose(0, 1, 3, 2)
    arranged = to_columns(arranged.reshape(2, extent, full_width))
    transfer = (arranged[0], arranged[1])
    norm_scale = 1.0 / (full_width * full_width)

    def spectrum(values):
        columns = columns_forward(values, outer_len, inner_len)
        stacked = to_columns(jnp.stack(columns).reshape(2, extent, full_width))
        return rows_forward_t((stacked[0], stacked[1]))

    def back_to_cells(spectral, real_only):
        stacked = to_rows(jnp.stack(rows_inverse_t(spectral)))
        shaped = (
            stacked[0].reshape(extent, outer_len, inner_len),
            stacked[1].reshape(extent, outer_len, inner_len),
        )
        return columns_inverse(shaped, outer_len, inner_len, real_only)

    mask_spec = spectrum((mask_level, None))
    field_val = back_to_cells(complex_mul(transfer, mask_spec), False)
    field_val = (field_val[0] * norm_scale, field_val[1] * norm_scale)
    intensity_term = weight * (field_val[0] * field_val[0] + field_val[1] * field_val[1])
    cotangent, resist = resist_section(intensity_term, blur_taps, target, kern_count, kern_index)
    factor = 2.0 * weight * cotangent
    carried_spec = spectrum((factor * field_val[0], factor * field_val[1]))
    gradient_term = (
        back_to_cells(complex_mul((transfer[0], -transfer[1]), carried_spec), True) * norm_scale
    )
    gradient = scatter_sum_cols(gradient_term, "kern")
    return (gradient, resist)


def solution(mesh):
    placed = (P("slab", None), P("kern", None, "slab", None), P(), P(), P(), P("slab", None))
    return jax.shard_map(
        on_device,
        mesh=mesh,
        in_specs=placed,
        out_specs=(P("slab", "kern"), P("slab", "kern")),
        check_vma=False,
    )
```

```python
import math

import jax
import jax.numpy as jnp
from jax import lax
from jax.sharding import PartitionSpec as P

CQ = 128


STEEP = 4.0
LEVEL = 0.5


def swapped(shard, axis, apart):
    return lax.ppermute(shard, axis, [(i, i ^ 1 << apart) for i in range(lax.axis_size(axis))])


def padded_2(shard, sides, width):
    for axis, dim in sides:
        devices, length = (lax.axis_size(axis), shard.shape[dim])
        up = [(i, (i + 1) % devices) for i in range(devices - 1)]
        down = [(j, i) for i, j in up]
        last = lax.slice_in_dim(shard, length - width, length, axis=dim)
        initial = lax.slice_in_dim(shard, 0, width, axis=dim)
        before = lax.ppermute(last, axis, up)
        after = lax.ppermute(initial, axis, down)
        shard = jnp.concatenate([before, shard, after], axis=dim)
    return shard


def reversed_bits(number, num_bits):
    result = number * 0
    for bit_pos in range(num_bits):
        result = result * 2 + number // 2**bit_pos % 2
    return result


def rotation(product, length, sign_val):
    fraction = (product % length).astype(jnp.float32) / length
    angles = sign_val * 2.0 * math.pi * fraction
    return (jnp.cos(angles), jnp.sin(angles))


def complex_mul(first_pair, second_pair):
    real_part = first_pair[0] * second_pair[0] - first_pair[1] * second_pair[1]
    imag_part = first_pair[0] * second_pair[1] + first_pair[1] * second_pair[0]
    return (real_part, imag_part)


def table_product(pattern, matrix, values):
    highest = lax.Precision.HIGHEST

    def single(first_op, second_op):
        return jnp.einsum(pattern, first_op, second_op, precision=highest)

    if values[1] is None:
        return (single(matrix[0], values[0]), single(matrix[1], values[0]))
    real_part = single(matrix[0], values[0]) - single(matrix[1], values[1])
    imag_part = single(matrix[0], values[1]) + single(matrix[1], values[0])
    return (real_part, imag_part)


def columns_forward(values, outer_len, inner_len):
    extent = values[0].shape[0]
    shaped = tuple(
        (None if piece is None else piece.reshape(extent, outer_len, inner_len) for piece in values)
    )
    outer_idx = jnp.arange(outer_len)
    inner_idx = jnp.arange(inner_len)
    section = table_product(
        "ab,rbq->raq", rotation(outer_idx[:, None] * outer_idx[None, :], outer_len, -1.0), shaped
    )
    section = complex_mul(
        section, rotation(outer_idx[:, None] * inner_idx[None, :], outer_len * inner_len, -1.0)
    )
    return table_product(
        "bk,rpb->rpk", rotation(inner_idx[:, None] * inner_idx[None, :], inner_len, -1.0), section
    )


def columns_inverse(values, outer_len, inner_len, real_only):
    extent = values[0].shape[0]
    outer_idx = jnp.arange(outer_len)
    inner_idx = jnp.arange(inner_len)
    section = table_product(
        "bk,rpb->rpk", rotation(inner_idx[:, None] * inner_idx[None, :], inner_len, 1.0), values
    )
    section = complex_mul(
        section, rotation(outer_idx[:, None] * inner_idx[None, :], outer_len * inner_len, 1.0)
    )
    matrix = rotation(outer_idx[:, None] * outer_idx[None, :], outer_len, 1.0)
    if real_only:
        highest = lax.Precision.HIGHEST
        real_part = jnp.einsum("ab,rbq->raq", matrix[0], section[0], precision=highest)
        real_part = real_part - jnp.einsum("ab,rbq->raq", matrix[1], section[1], precision=highest)
        return real_part.reshape(extent, outer_len * inner_len)
    result = table_product("ab,rbq->raq", matrix, section)
    return (
        result[0].reshape(extent, outer_len * inner_len),
        result[1].reshape(extent, outer_len * inner_len),
    )


def rows_forward(values, freq_offset, full_width):
    extent = values[0].shape[0]
    positions = jnp.arange(extent)
    twiddle = rotation(positions * freq_offset, full_width, -1.0)
    values = complex_mul(values, (twiddle[0][:, None], twiddle[1][:, None]))
    return table_product(
        "sr,rc->sc", rotation(positions[:, None] * positions[None, :], extent, -1.0), values
    )


def rows_inverse(values, freq_offset, full_width):
    extent = values[0].shape[0]
    positions = jnp.arange(extent)
    values = table_product(
        "rs,sc->rc", rotation(positions[:, None] * positions[None, :], extent, 1.0), values
    )
    twiddle = rotation(positions * freq_offset, full_width, 1.0)
    return complex_mul(values, (twiddle[0][:, None], twiddle[1][:, None]))


def pairs_forward(stacked, num_bits):
    slab_index = lax.axis_index("slab")
    for bit_level in range(num_bits - 1, -1, -1):
        half_span = 2**bit_level
        partner = swapped(stacked, "slab", bit_level)
        is_upper = slab_index // half_span % 2 == 1
        twiddle = rotation(slab_index % half_span, 2 * half_span, -1.0)
        lower_val = stacked + partner
        difference = partner - stacked
        upper_val = jnp.stack(complex_mul((difference[0], difference[1]), twiddle))
        stacked = jnp.where(is_upper, upper_val, lower_val)
    return stacked


def pairs_inverse(stacked, num_bits):
    slab_index = lax.axis_index("slab")
    for bit_level in range(num_bits):
        half_span = 2**bit_level
        partner = swapped(stacked, "slab", bit_level)
        is_upper = slab_index // half_span % 2 == 1
        twiddle = rotation(slab_index % half_span, 2 * half_span, 1.0)
        from_upper = jnp.where(is_upper, stacked, partner)
        from_lower = jnp.where(is_upper, partner, stacked)
        turned = jnp.stack(complex_mul((from_upper[0], from_upper[1]), twiddle))
        stacked = jnp.where(is_upper, from_lower - turned, from_lower + turned)
    return stacked


def mix_forward(stacked, num_bits):
    return pairs_forward(stacked, num_bits)


def mix_inverse(stacked, num_bits):
    return pairs_inverse(stacked, num_bits)


def tap_band(kernel_taps, rows, cols, offset):
    diff = jnp.arange(rows)[:, None] - jnp.arange(cols)[None, :] - offset
    tap_idx = jnp.arange(kernel_taps.shape[0])[:, None, None]
    hits = jnp.where(diff[None] == tap_idx, kernel_taps[:, None, None], 0.0)
    return jnp.sum(hits, axis=0)


def blur_bands(kernel_taps, extent, block, margin):
    reach = (kernel_taps.shape[0] - 1) // 2
    row_band = tap_band(kernel_taps, extent + 2 * reach, extent, 0).T
    col_band = tap_band(kernel_taps, block + 2 * margin, block, margin - reach)
    return (row_band, col_band)


def smooth(padded, bands, extent, span):
    highest = lax.Precision.HIGHEST
    row_band, col_band = bands
    row_part = jnp.dot(row_band, padded, precision=highest)
    block = col_band.shape[1]
    margin = (col_band.shape[0] - block) // 2
    widened = jnp.pad(row_part, ((0, 0), (margin, margin)))
    windows = jnp.stack(
        [widened[:, j * block : j * block + block + 2 * margin] for j in range(span // block)], 1
    )
    result = jnp.einsum("rji,ib->rjb", windows, col_band, precision=highest)
    return result.reshape(extent, span)


def exchanged(shard, axis, offset):
    return lax.ppermute(shard, axis, [(i, i ^ offset) for i in range(lax.axis_size(axis))])


def digit_groups(count, radix):
    groups = []
    while count > 1:
        groups.append(min(radix, count))
        count //= min(radix, count)
    return groups


def reduce_scatter_cols(values, axis, radix=4):
    count = lax.axis_size(axis)
    index = lax.axis_index(axis)
    extent, width = values.shape
    groups = digit_groups(count, radix)
    values = values.reshape((extent,) + tuple(reversed(groups)) + (width // count,))
    stride = 1
    for level, size in enumerate(groups):
        dim = len(groups) - level
        mine = index // stride % size
        total = lax.dynamic_index_in_dim(values, mine, axis=dim, keepdims=False)
        for offset in range(1, size):
            send = lax.dynamic_index_in_dim(values, mine ^ offset, axis=dim, keepdims=False)
            total = total + exchanged(send, axis, offset * stride)
        values = total
        stride *= size
    return values.reshape(extent, width // count)


def all_gather_cols(values, axis, radix=4):
    count = lax.axis_size(axis)
    index = lax.axis_index(axis)
    extent, block = values.shape
    groups = digit_groups(count, radix)
    stride = count
    for size in reversed(groups):
        stride //= size
        mine = index // stride % size
        got = [values] + [exchanged(values, axis, offset * stride) for offset in range(1, size)]
        parts = []
        for slot in range(size):
            part = jnp.zeros_like(values)
            for offset in range(size):
                part = part + jnp.where((slot ^ mine) == offset, got[offset], 0.0)
            parts.append(part)
        values = jnp.stack(parts, values.ndim - 1)
    return values.reshape(extent, block * count)


def scatter_sum_cols(values, axis):
    count = lax.axis_size(axis)
    extent, width = values.shape
    share = width // count
    split = values.reshape(extent, count, share).transpose(1, 0, 2)
    split = split.reshape(count, extent * share // 128, 128)
    joined = lax.all_to_all(split, axis, 0, 0, tiled=True)
    return jnp.sum(joined, axis=0).reshape(extent, share)


def gather_cols(values, axis):
    count = lax.axis_size(axis)
    extent, share = values.shape
    copies = jnp.broadcast_to(values.reshape(1, extent * share // 128, 128), (count, extent * share // 128, 128))
    joined = lax.all_to_all(copies, axis, 0, 0, tiled=True).reshape(count, extent, share)
    return joined.transpose(1, 0, 2).reshape(extent, count * share)


def all_reduce_cols(values, axis, widen, radix=4):
    count = lax.axis_size(axis)
    index = lax.axis_index(axis)
    low = min(radix, count)
    high = count // low
    extent, width = values.shape
    values = values.reshape(extent, high, low, width // count)
    mine = index % low
    total = lax.dynamic_index_in_dim(values, mine, axis=2, keepdims=False)
    for offset in range(1, low):
        send = lax.dynamic_index_in_dim(values, mine ^ offset, axis=2, keepdims=False)
        total = total + exchanged(send, axis, offset)
    upper = index // low
    got = [total] + [exchanged(total, axis, offset * low) for offset in range(1, high)]
    summed = jnp.zeros_like(total)
    for slot in range(high):
        term = jnp.zeros_like(total)
        for offset in range(high):
            term = term + jnp.where((slot ^ upper) == offset, got[offset], 0.0)
        summed = summed + term
    summed = widen(summed)
    got = [summed] + [exchanged(summed, axis, offset) for offset in range(1, low)]
    parts = []
    for slot in range(low):
        part = jnp.zeros_like(summed)
        for offset in range(low):
            part = part + jnp.where((slot ^ mine) == offset, got[offset], 0.0)
        parts.append(part)
    return jnp.stack(parts, 2).reshape(summed.shape[0], width)


def resist_section(intensity_term, kernel_taps, target, kern_count, kern_index):
    reach = (kernel_taps.shape[0] - 1) // 2
    flipped = kernel_taps[::-1]
    extent, full_width = intensity_term.shape
    share_cols = full_width // kern_count
    wide = extent + 2 * reach
    bands = lax.optimization_barrier(
        (blur_bands(kernel_taps, wide, 128, 64), blur_bands(flipped, extent, 128, 64))
    )
    goal_cells = padded_2(target, (("slab", 0),), reach).astype(jnp.float32)
    block = padded_2(scatter_sum_cols(intensity_term, "kern"), (("slab", 0),), 2 * reach)
    summed = gather_cols(block, "kern")
    resist = jax.nn.sigmoid(STEEP * (smooth(summed, bands[0], wide, full_width) - LEVEL))
    first_row = lax.axis_index("slab") * extent - reach
    rows = first_row + jnp.arange(wide)
    inside = (rows >= 0) & (rows < lax.axis_size("slab") * extent)
    slope_grad = 2.0 * (resist - goal_cells) * STEEP * resist * (1.0 - resist)
    slope_grad = jnp.where(inside[:, None], slope_grad, 0.0)
    cotangent = smooth(slope_grad, bands[1], extent, full_width)
    resist = lax.dynamic_slice_in_dim(resist[reach : reach + extent], kern_index * share_cols, share_cols, 1)
    return (cotangent, resist)


def to_columns(stacked):
    pieces, extent, width = stacked.shape
    count = lax.axis_size("slab")
    share = width // count
    split = stacked.reshape(pieces, extent, count, share).transpose(2, 0, 1, 3)
    split = split.reshape(count, pieces * extent * share // 128, 128)
    joined = lax.all_to_all(split, "slab", 0, 0, tiled=True)
    return joined.reshape(count, pieces, extent, share).transpose(1, 0, 2, 3)


def to_rows(stacked):
    pieces, count, extent, share = stacked.shape
    split = stacked.transpose(1, 0, 2, 3).reshape(count, pieces * extent * share // 128, 128)
    joined = lax.all_to_all(split, "slab", 0, 0, tiled=True).reshape(count, pieces, extent, share)
    return joined.transpose(1, 2, 0, 3).reshape(pieces, extent, count * share)


def row_tables(count, extent, sign_val):
    num_bits = count.bit_length() - 1
    slab_idx = jnp.arange(count)
    local_idx = jnp.arange(extent)
    flipped = reversed_bits(slab_idx, num_bits)
    across = rotation(flipped[:, None] * slab_idx[None, :], count, sign_val)
    twiddle = rotation(flipped[:, None] * local_idx[None, :], count * extent, sign_val)
    within = rotation(local_idx[:, None] * local_idx[None, :], extent, sign_val)
    return (across, twiddle, within)


def rows_forward_t(values):
    count, extent, _ = values[0].shape
    across, twiddle, within = row_tables(count, extent, -1.0)
    values = table_product("ed,dpv->epv", across, values)
    values = complex_mul(values, (twiddle[0][:, :, None], twiddle[1][:, :, None]))
    return table_product("qp,epv->eqv", within, values)


def rows_inverse_t(values):
    count, extent, _ = values[0].shape
    across, twiddle, within = row_tables(count, extent, 1.0)
    values = table_product("pq,eqv->epv", within, values)
    values = complex_mul(values, (twiddle[0][:, :, None], twiddle[1][:, :, None]))
    return table_product("ed,epv->dpv", across, values)


def on_device(mask_level, kernel_spectra, socs_weight, kernel_slot, blur_taps, target):
    extent, full_width = mask_level.shape
    slab_count = lax.axis_size("slab")
    kern_count = lax.axis_size("kern")
    num_bits = slab_count.bit_length() - 1
    inner_len = CQ
    outer_len = full_width // inner_len
    freq_offset = reversed_bits(lax.axis_index("slab"), num_bits)
    kern_index = lax.axis_index("kern")
    kernel_id = jnp.sum(jnp.where(jnp.arange(kernel_slot.shape[0]) == kern_index, kernel_slot, 0))
    weight = jnp.sum(jnp.where(jnp.arange(socs_weight.shape[0]) == kernel_id, socs_weight, 0.0))
    arranged = kernel_spectra[0].reshape(2, extent, inner_len, outer_len).transpose(0, 1, 3, 2)
    arranged = to_columns(arranged.reshape(2, extent, full_width))
    transfer = (arranged[0], arranged[1])
    norm_scale = 1.0 / (full_width * full_width)

    def spectrum(values):
        columns = columns_forward(values, outer_len, inner_len)
        stacked = to_columns(jnp.stack(columns).reshape(2, extent, full_width))
        return rows_forward_t((stacked[0], stacked[1]))

    def back_to_cells(spectral, real_only):
        stacked = to_rows(jnp.stack(rows_inverse_t(spectral)))
        shaped = (
            stacked[0].reshape(extent, outer_len, inner_len),
            stacked[1].reshape(extent, outer_len, inner_len),
        )
        return columns_inverse(shaped, outer_len, inner_len, real_only)

    mask_spec = spectrum((mask_level, None))
    field_val = back_to_cells(complex_mul(transfer, mask_spec), False)
    field_val = (field_val[0] * norm_scale, field_val[1] * norm_scale)
    intensity_term = weight * (field_val[0] * field_val[0] + field_val[1] * field_val[1])
    cotangent, resist = resist_section(intensity_term, blur_taps, target, kern_count, kern_index)
    factor = 2.0 * weight * cotangent
    carried_spec = spectrum((factor * field_val[0], factor * field_val[1]))
    gradient_term = (
        back_to_cells(complex_mul((transfer[0], -transfer[1]), carried_spec), True) * norm_scale
    )
    gradient = scatter_sum_cols(gradient_term, "kern")
    return (gradient, resist)


def solution(mesh):
    placed = (P("slab", None), P("kern", None, "slab", None), P(), P(), P(), P("slab", None))
    return jax.shard_map(
        on_device,
        mesh=mesh,
        in_specs=placed,
        out_specs=(P("slab", "kern"), P("slab", "kern")),
        check_vma=False,
    )
```

```python
import math

import jax
import numpy as np
import jax.numpy as jnp
from jax import lax
from jax.sharding import PartitionSpec as P

CQ = 128


STEEP = 4.0
LEVEL = 0.5


def swapped(shard, axis, apart):
    return lax.ppermute(shard, axis, [(i, i ^ 1 << apart) for i in range(lax.axis_size(axis))])


def padded_2(shard, sides, width):
    for axis, dim in sides:
        devices, length = (lax.axis_size(axis), shard.shape[dim])
        up = [(i, (i + 1) % devices) for i in range(devices - 1)]
        down = [(j, i) for i, j in up]
        last = lax.slice_in_dim(shard, length - width, length, axis=dim)
        initial = lax.slice_in_dim(shard, 0, width, axis=dim)
        before = lax.ppermute(last, axis, up)
        after = lax.ppermute(initial, axis, down)
        shard = jnp.concatenate([before, shard, after], axis=dim)
    return shard


def reversed_bits(number, num_bits):
    result = number * 0
    for bit_pos in range(num_bits):
        result = result * 2 + number // 2**bit_pos % 2
    return result


def rotation(product, length, sign_val):
    if isinstance(product, np.ndarray):
        angles = sign_val * 2.0 * np.pi * (product % length) / length
        return (jnp.asarray(np.cos(angles), jnp.float32), jnp.asarray(np.sin(angles), jnp.float32))
    fraction = (product % length).astype(jnp.float32) / length
    angles = sign_val * 2.0 * math.pi * fraction
    return (jnp.cos(angles), jnp.sin(angles))


def complex_mul(first_pair, second_pair):
    real_part = first_pair[0] * second_pair[0] - first_pair[1] * second_pair[1]
    imag_part = first_pair[0] * second_pair[1] + first_pair[1] * second_pair[0]
    return (real_part, imag_part)


def table_product(pattern, matrix, values):
    highest = lax.Precision.HIGHEST

    def single(first_op, second_op):
        return jnp.einsum(pattern, first_op, second_op, precision=highest)

    if values[1] is None:
        return (single(matrix[0], values[0]), single(matrix[1], values[0]))
    real_part = single(matrix[0], values[0]) - single(matrix[1], values[1])
    imag_part = single(matrix[0], values[1]) + single(matrix[1], values[0])
    return (real_part, imag_part)


def columns_forward(values, outer_len, inner_len):
    extent = values[0].shape[0]
    shaped = tuple(
        (None if piece is None else piece.reshape(extent, outer_len, inner_len) for piece in values)
    )
    outer_idx = np.arange(outer_len)
    inner_idx = np.arange(inner_len)
    section = table_product(
        "ab,rbq->raq", rotation(outer_idx[:, None] * outer_idx[None, :], outer_len, -1.0), shaped
    )
    section = complex_mul(
        section, rotation(outer_idx[:, None] * inner_idx[None, :], outer_len * inner_len, -1.0)
    )
    return table_product(
        "bk,rpb->rpk", rotation(inner_idx[:, None] * inner_idx[None, :], inner_len, -1.0), section
    )


def columns_inverse(values, outer_len, inner_len, real_only):
    extent = values[0].shape[0]
    outer_idx = np.arange(outer_len)
    inner_idx = np.arange(inner_len)
    section = table_product(
        "bk,rpb->rpk", rotation(inner_idx[:, None] * inner_idx[None, :], inner_len, 1.0), values
    )
    section = complex_mul(
        section, rotation(outer_idx[:, None] * inner_idx[None, :], outer_len * inner_len, 1.0)
    )
    matrix = rotation(outer_idx[:, None] * outer_idx[None, :], outer_len, 1.0)
    if real_only:
        highest = lax.Precision.HIGHEST
        real_part = jnp.einsum("ab,rbq->raq", matrix[0], section[0], precision=highest)
        real_part = real_part - jnp.einsum("ab,rbq->raq", matrix[1], section[1], precision=highest)
        return real_part.reshape(extent, outer_len * inner_len)
    result = table_product("ab,rbq->raq", matrix, section)
    return (
        result[0].reshape(extent, outer_len * inner_len),
        result[1].reshape(extent, outer_len * inner_len),
    )


def rows_forward(values, freq_offset, full_width):
    extent = values[0].shape[0]
    positions = jnp.arange(extent)
    twiddle = rotation(positions * freq_offset, full_width, -1.0)
    values = complex_mul(values, (twiddle[0][:, None], twiddle[1][:, None]))
    return table_product(
        "sr,rc->sc", rotation(positions[:, None] * positions[None, :], extent, -1.0), values
    )


def rows_inverse(values, freq_offset, full_width):
    extent = values[0].shape[0]
    positions = jnp.arange(extent)
    values = table_product(
        "rs,sc->rc", rotation(positions[:, None] * positions[None, :], extent, 1.0), values
    )
    twiddle = rotation(positions * freq_offset, full_width, 1.0)
    return complex_mul(values, (twiddle[0][:, None], twiddle[1][:, None]))


def pairs_forward(stacked, num_bits):
    slab_index = lax.axis_index("slab")
    for bit_level in range(num_bits - 1, -1, -1):
        half_span = 2**bit_level
        partner = swapped(stacked, "slab", bit_level)
        is_upper = slab_index // half_span % 2 == 1
        twiddle = rotation(slab_index % half_span, 2 * half_span, -1.0)
        lower_val = stacked + partner
        difference = partner - stacked
        upper_val = jnp.stack(complex_mul((difference[0], difference[1]), twiddle))
        stacked = jnp.where(is_upper, upper_val, lower_val)
    return stacked


def pairs_inverse(stacked, num_bits):
    slab_index = lax.axis_index("slab")
    for bit_level in range(num_bits):
        half_span = 2**bit_level
        partner = swapped(stacked, "slab", bit_level)
        is_upper = slab_index // half_span % 2 == 1
        twiddle = rotation(slab_index % half_span, 2 * half_span, 1.0)
        from_upper = jnp.where(is_upper, stacked, partner)
        from_lower = jnp.where(is_upper, partner, stacked)
        turned = jnp.stack(complex_mul((from_upper[0], from_upper[1]), twiddle))
        stacked = jnp.where(is_upper, from_lower - turned, from_lower + turned)
    return stacked


def mix_forward(stacked, num_bits):
    return pairs_forward(stacked, num_bits)


def mix_inverse(stacked, num_bits):
    return pairs_inverse(stacked, num_bits)


def tap_band(kernel_taps, rows, cols, offset):
    diff = jnp.arange(rows)[:, None] - jnp.arange(cols)[None, :] - offset
    tap_idx = jnp.arange(kernel_taps.shape[0])[:, None, None]
    hits = jnp.where(diff[None] == tap_idx, kernel_taps[:, None, None], 0.0)
    return jnp.sum(hits, axis=0)


def blur_bands(kernel_taps, extent, block, margin):
    reach = (kernel_taps.shape[0] - 1) // 2
    row_band = tap_band(kernel_taps, extent + 2 * reach, extent, 0).T
    col_band = tap_band(kernel_taps, block + 2 * margin, block, margin - reach)
    return (row_band, col_band)


def smooth(padded, bands, extent, span):
    highest = lax.Precision.HIGHEST
    row_band, col_band = bands
    row_part = jnp.dot(row_band, padded, precision=highest)
    block = col_band.shape[1]
    margin = (col_band.shape[0] - block) // 2
    widened = jnp.pad(row_part, ((0, 0), (margin, margin)))
    windows = jnp.stack(
        [widened[:, j * block : j * block + block + 2 * margin] for j in range(span // block)], 1
    )
    result = jnp.einsum("rji,ib->rjb", windows, col_band, precision=highest)
    return result.reshape(extent, span)


def exchanged(shard, axis, offset):
    return lax.ppermute(shard, axis, [(i, i ^ offset) for i in range(lax.axis_size(axis))])


def digit_groups(count, radix):
    groups = []
    while count > 1:
        groups.append(min(radix, count))
        count //= min(radix, count)
    return groups


def reduce_scatter_cols(values, axis, radix=4):
    count = lax.axis_size(axis)
    index = lax.axis_index(axis)
    extent, width = values.shape
    groups = digit_groups(count, radix)
    values = values.reshape((extent,) + tuple(reversed(groups)) + (width // count,))
    stride = 1
    for level, size in enumerate(groups):
        dim = len(groups) - level
        mine = index // stride % size
        total = lax.dynamic_index_in_dim(values, mine, axis=dim, keepdims=False)
        for offset in range(1, size):
            send = lax.dynamic_index_in_dim(values, mine ^ offset, axis=dim, keepdims=False)
            total = total + exchanged(send, axis, offset * stride)
        values = total
        stride *= size
    return values.reshape(extent, width // count)


def all_gather_cols(values, axis, radix=4):
    count = lax.axis_size(axis)
    index = lax.axis_index(axis)
    extent, block = values.shape
    groups = digit_groups(count, radix)
    stride = count
    for size in reversed(groups):
        stride //= size
        mine = index // stride % size
        got = [values] + [exchanged(values, axis, offset * stride) for offset in range(1, size)]
        parts = []
        for slot in range(size):
            part = jnp.zeros_like(values)
            for offset in range(size):
                part = part + jnp.where((slot ^ mine) == offset, got[offset], 0.0)
            parts.append(part)
        values = jnp.stack(parts, values.ndim - 1)
    return values.reshape(extent, block * count)


def scatter_sum_cols(values, axis):
    count = lax.axis_size(axis)
    extent, width = values.shape
    share = width // count
    split = values.reshape(extent, count, share).transpose(1, 0, 2)
    split = split.reshape(count, extent * share // 128, 128)
    joined = lax.all_to_all(split, axis, 0, 0, tiled=True)
    return jnp.sum(joined, axis=0).reshape(extent, share)


def all_reduce_cols(values, axis, widen, radix=4):
    count = lax.axis_size(axis)
    index = lax.axis_index(axis)
    low = min(radix, count)
    high = count // low
    extent, width = values.shape
    values = values.reshape(extent, high, low, width // count)
    mine = index % low
    total = lax.dynamic_index_in_dim(values, mine, axis=2, keepdims=False)
    for offset in range(1, low):
        send = lax.dynamic_index_in_dim(values, mine ^ offset, axis=2, keepdims=False)
        total = total + exchanged(send, axis, offset)
    upper = index // low
    got = [total] + [exchanged(total, axis, offset * low) for offset in range(1, high)]
    summed = jnp.zeros_like(total)
    for slot in range(high):
        term = jnp.zeros_like(total)
        for offset in range(high):
            term = term + jnp.where((slot ^ upper) == offset, got[offset], 0.0)
        summed = summed + term
    summed = widen(summed)
    got = [summed] + [exchanged(summed, axis, offset) for offset in range(1, low)]
    parts = []
    for slot in range(low):
        part = jnp.zeros_like(summed)
        for offset in range(low):
            part = part + jnp.where((slot ^ mine) == offset, got[offset], 0.0)
        parts.append(part)
    return jnp.stack(parts, 2).reshape(summed.shape[0], width)


def resist_section(intensity_term, kernel_taps, target, kern_count, kern_index):
    reach = (kernel_taps.shape[0] - 1) // 2
    flipped = kernel_taps[::-1]
    extent, full_width = intensity_term.shape
    share_cols = full_width // kern_count
    wide = extent + 2 * reach
    bands = lax.optimization_barrier(
        (blur_bands(kernel_taps, wide, 128, 64), blur_bands(flipped, extent, 128, 64))
    )
    goal_cells = padded_2(target, (("slab", 0),), reach).astype(jnp.float32)
    summed = all_reduce_cols(
        intensity_term, "kern", lambda block: padded_2(block, (("slab", 0),), 2 * reach)
    )
    resist = jax.nn.sigmoid(STEEP * (smooth(summed, bands[0], wide, full_width) - LEVEL))
    first_row = lax.axis_index("slab") * extent - reach
    rows = first_row + jnp.arange(wide)
    inside = (rows >= 0) & (rows < lax.axis_size("slab") * extent)
    slope_grad = 2.0 * (resist - goal_cells) * STEEP * resist * (1.0 - resist)
    slope_grad = jnp.where(inside[:, None], slope_grad, 0.0)
    cotangent = smooth(slope_grad, bands[1], extent, full_width)
    resist = lax.dynamic_slice_in_dim(resist[reach : reach + extent], kern_index * share_cols, share_cols, 1)
    return (cotangent, resist)


def to_columns(stacked):
    pieces, extent, width = stacked.shape
    count = lax.axis_size("slab")
    share = width // count
    split = stacked.reshape(pieces, extent, count, share).transpose(2, 0, 1, 3)
    split = split.reshape(count, pieces * extent * share // 128, 128)
    joined = lax.all_to_all(split, "slab", 0, 0, tiled=True)
    return joined.reshape(count, pieces, extent, share).transpose(1, 0, 2, 3)


def to_rows(stacked):
    pieces, count, extent, share = stacked.shape
    split = stacked.transpose(1, 0, 2, 3).reshape(count, pieces * extent * share // 128, 128)
    joined = lax.all_to_all(split, "slab", 0, 0, tiled=True).reshape(count, pieces, extent, share)
    return joined.transpose(1, 2, 0, 3).reshape(pieces, extent, count * share)


def row_tables(count, extent, sign_val):
    num_bits = count.bit_length() - 1
    slab_idx = np.arange(count)
    local_idx = np.arange(extent)
    flipped = reversed_bits(slab_idx, num_bits)
    across = rotation(flipped[:, None] * slab_idx[None, :], count, sign_val)
    twiddle = rotation(flipped[:, None] * local_idx[None, :], count * extent, sign_val)
    within = rotation(local_idx[:, None] * local_idx[None, :], extent, sign_val)
    return (across, twiddle, within)


def rows_forward_t(values):
    count, extent, _ = values[0].shape
    across, twiddle, within = row_tables(count, extent, -1.0)
    values = table_product("ed,dpv->epv", across, values)
    values = complex_mul(values, (twiddle[0][:, :, None], twiddle[1][:, :, None]))
    return table_product("qp,epv->eqv", within, values)


def rows_inverse_t(values):
    count, extent, _ = values[0].shape
    across, twiddle, within = row_tables(count, extent, 1.0)
    values = table_product("pq,eqv->epv", within, values)
    values = complex_mul(values, (twiddle[0][:, :, None], twiddle[1][:, :, None]))
    return table_product("ed,epv->dpv", across, values)


def on_device(mask_level, kernel_spectra, socs_weight, kernel_slot, blur_taps, target):
    extent, full_width = mask_level.shape
    slab_count = lax.axis_size("slab")
    kern_count = lax.axis_size("kern")
    num_bits = slab_count.bit_length() - 1
    inner_len = CQ
    outer_len = full_width // inner_len
    freq_offset = reversed_bits(lax.axis_index("slab"), num_bits)
    kern_index = lax.axis_index("kern")
    kernel_id = jnp.sum(jnp.where(jnp.arange(kernel_slot.shape[0]) == kern_index, kernel_slot, 0))
    weight = jnp.sum(jnp.where(jnp.arange(socs_weight.shape[0]) == kernel_id, socs_weight, 0.0))
    arranged = kernel_spectra[0].reshape(2, extent, inner_len, outer_len).transpose(0, 1, 3, 2)
    arranged = to_columns(arranged.reshape(2, extent, full_width))
    transfer = (arranged[0], arranged[1])
    norm_scale = 1.0 / (full_width * full_width)

    def spectrum(values):
        columns = columns_forward(values, outer_len, inner_len)
        stacked = to_columns(jnp.stack(columns).reshape(2, extent, full_width))
        return rows_forward_t((stacked[0], stacked[1]))

    def back_to_cells(spectral, real_only):
        stacked = to_rows(jnp.stack(rows_inverse_t(spectral)))
        shaped = (
            stacked[0].reshape(extent, outer_len, inner_len),
            stacked[1].reshape(extent, outer_len, inner_len),
        )
        return columns_inverse(shaped, outer_len, inner_len, real_only)

    mask_spec = spectrum((mask_level, None))
    field_val = back_to_cells(complex_mul(transfer, mask_spec), False)
    field_val = (field_val[0] * norm_scale, field_val[1] * norm_scale)
    intensity_term = weight * (field_val[0] * field_val[0] + field_val[1] * field_val[1])
    cotangent, resist = resist_section(intensity_term, blur_taps, target, kern_count, kern_index)
    factor = 2.0 * weight * cotangent
    carried_spec = spectrum((factor * field_val[0], factor * field_val[1]))
    gradient_term = (
        back_to_cells(complex_mul((transfer[0], -transfer[1]), carried_spec), True) * norm_scale
    )
    gradient = scatter_sum_cols(gradient_term, "kern")
    return (gradient, resist)


def solution(mesh):
    placed = (P("slab", None), P("kern", None, "slab", None), P(), P(), P(), P("slab", None))
    return jax.shard_map(
        on_device,
        mesh=mesh,
        in_specs=placed,
        out_specs=(P("slab", "kern"), P("slab", "kern")),
        check_vma=False,
    )
```

```python
import math

import jax
import numpy as np
import jax.numpy as jnp
from jax import lax
from jax.sharding import PartitionSpec as P

CQ = 128


STEEP = 4.0
LEVEL = 0.5


def swapped(shard, axis, apart):
    return lax.ppermute(shard, axis, [(i, i ^ 1 << apart) for i in range(lax.axis_size(axis))])


def padded_2(shard, sides, width):
    for axis, dim in sides:
        devices, length = (lax.axis_size(axis), shard.shape[dim])
        up = [(i, (i + 1) % devices) for i in range(devices - 1)]
        down = [(j, i) for i, j in up]
        last = lax.slice_in_dim(shard, length - width, length, axis=dim)
        initial = lax.slice_in_dim(shard, 0, width, axis=dim)
        before = lax.ppermute(last, axis, up)
        after = lax.ppermute(initial, axis, down)
        shard = jnp.concatenate([before, shard, after], axis=dim)
    return shard


def reversed_bits(number, num_bits):
    result = number * 0
    for bit_pos in range(num_bits):
        result = result * 2 + number // 2**bit_pos % 2
    return result


def rotation(product, length, sign_val):
    if isinstance(product, np.ndarray):
        angles = sign_val * 2.0 * np.pi * (product % length) / length
        return (jnp.asarray(np.cos(angles), jnp.float32), jnp.asarray(np.sin(angles), jnp.float32))
    fraction = (product % length).astype(jnp.float32) / length
    angles = sign_val * 2.0 * math.pi * fraction
    return (jnp.cos(angles), jnp.sin(angles))


def complex_mul(first_pair, second_pair):
    real_part = first_pair[0] * second_pair[0] - first_pair[1] * second_pair[1]
    imag_part = first_pair[0] * second_pair[1] + first_pair[1] * second_pair[0]
    return (real_part, imag_part)


def table_product(pattern, matrix, values):
    highest = lax.Precision.HIGHEST

    def single(first_op, second_op):
        return jnp.einsum(pattern, first_op, second_op, precision=highest)

    if values[1] is None:
        return (single(matrix[0], values[0]), single(matrix[1], values[0]))
    real_part = single(matrix[0], values[0]) - single(matrix[1], values[1])
    imag_part = single(matrix[0], values[1]) + single(matrix[1], values[0])
    return (real_part, imag_part)


def columns_forward(values, outer_len, inner_len):
    extent = values[0].shape[0]
    shaped = tuple(
        (None if piece is None else piece.reshape(extent, outer_len, inner_len) for piece in values)
    )
    outer_idx = np.arange(outer_len)
    inner_idx = np.arange(inner_len)
    section = table_product(
        "ab,rbq->raq", rotation(outer_idx[:, None] * outer_idx[None, :], outer_len, -1.0), shaped
    )
    section = complex_mul(
        section, rotation(outer_idx[:, None] * inner_idx[None, :], outer_len * inner_len, -1.0)
    )
    return table_product(
        "bk,rpb->rpk", rotation(inner_idx[:, None] * inner_idx[None, :], inner_len, -1.0), section
    )


def columns_inverse(values, outer_len, inner_len, real_only, scale=1.0):
    extent = values[0].shape[0]
    outer_idx = np.arange(outer_len)
    inner_idx = np.arange(inner_len)
    section = table_product(
        "bk,rpb->rpk", rotation(inner_idx[:, None] * inner_idx[None, :], inner_len, 1.0), values
    )
    section = complex_mul(
        section, rotation(outer_idx[:, None] * inner_idx[None, :], outer_len * inner_len, 1.0)
    )
    matrix = rotation(outer_idx[:, None] * outer_idx[None, :], outer_len, 1.0)
    matrix = (matrix[0] * scale, matrix[1] * scale)
    if real_only:
        highest = lax.Precision.HIGHEST
        real_part = jnp.einsum("ab,rbq->raq", matrix[0], section[0], precision=highest)
        real_part = real_part - jnp.einsum("ab,rbq->raq", matrix[1], section[1], precision=highest)
        return real_part.reshape(extent, outer_len * inner_len)
    result = table_product("ab,rbq->raq", matrix, section)
    return (
        result[0].reshape(extent, outer_len * inner_len),
        result[1].reshape(extent, outer_len * inner_len),
    )


def rows_forward(values, freq_offset, full_width):
    extent = values[0].shape[0]
    positions = jnp.arange(extent)
    twiddle = rotation(positions * freq_offset, full_width, -1.0)
    values = complex_mul(values, (twiddle[0][:, None], twiddle[1][:, None]))
    return table_product(
        "sr,rc->sc", rotation(positions[:, None] * positions[None, :], extent, -1.0), values
    )


def rows_inverse(values, freq_offset, full_width):
    extent = values[0].shape[0]
    positions = jnp.arange(extent)
    values = table_product(
        "rs,sc->rc", rotation(positions[:, None] * positions[None, :], extent, 1.0), values
    )
    twiddle = rotation(positions * freq_offset, full_width, 1.0)
    return complex_mul(values, (twiddle[0][:, None], twiddle[1][:, None]))


def pairs_forward(stacked, num_bits):
    slab_index = lax.axis_index("slab")
    for bit_level in range(num_bits - 1, -1, -1):
        half_span = 2**bit_level
        partner = swapped(stacked, "slab", bit_level)
        is_upper = slab_index // half_span % 2 == 1
        twiddle = rotation(slab_index % half_span, 2 * half_span, -1.0)
        lower_val = stacked + partner
        difference = partner - stacked
        upper_val = jnp.stack(complex_mul((difference[0], difference[1]), twiddle))
        stacked = jnp.where(is_upper, upper_val, lower_val)
    return stacked


def pairs_inverse(stacked, num_bits):
    slab_index = lax.axis_index("slab")
    for bit_level in range(num_bits):
        half_span = 2**bit_level
        partner = swapped(stacked, "slab", bit_level)
        is_upper = slab_index // half_span % 2 == 1
        twiddle = rotation(slab_index % half_span, 2 * half_span, 1.0)
        from_upper = jnp.where(is_upper, stacked, partner)
        from_lower = jnp.where(is_upper, partner, stacked)
        turned = jnp.stack(complex_mul((from_upper[0], from_upper[1]), twiddle))
        stacked = jnp.where(is_upper, from_lower - turned, from_lower + turned)
    return stacked


def mix_forward(stacked, num_bits):
    return pairs_forward(stacked, num_bits)


def mix_inverse(stacked, num_bits):
    return pairs_inverse(stacked, num_bits)


def tap_band(kernel_taps, rows, cols, offset):
    diff = jnp.arange(rows)[:, None] - jnp.arange(cols)[None, :] - offset
    tap_idx = jnp.arange(kernel_taps.shape[0])[:, None, None]
    hits = jnp.where(diff[None] == tap_idx, kernel_taps[:, None, None], 0.0)
    return jnp.sum(hits, axis=0)


def blur_bands(kernel_taps, extent, block, margin):
    reach = (kernel_taps.shape[0] - 1) // 2
    row_band = tap_band(kernel_taps, extent + 2 * reach, extent, 0).T
    col_band = tap_band(kernel_taps, block + 2 * margin, block, margin - reach)
    return (row_band, col_band)


def smooth(padded, bands, extent, span):
    highest = lax.Precision.HIGHEST
    row_band, col_band = bands
    row_part = jnp.dot(row_band, padded, precision=highest)
    block = col_band.shape[1]
    margin = (col_band.shape[0] - block) // 2
    widened = jnp.pad(row_part, ((0, 0), (margin, margin)))
    windows = jnp.stack(
        [widened[:, j * block : j * block + block + 2 * margin] for j in range(span // block)], 1
    )
    result = jnp.einsum("rji,ib->rjb", windows, col_band, precision=highest)
    return result.reshape(extent, span)


def exchanged(shard, axis, offset):
    return lax.ppermute(shard, axis, [(i, i ^ offset) for i in range(lax.axis_size(axis))])


def digit_groups(count, radix):
    groups = []
    while count > 1:
        groups.append(min(radix, count))
        count //= min(radix, count)
    return groups


def reduce_scatter_cols(values, axis, radix=4):
    count = lax.axis_size(axis)
    index = lax.axis_index(axis)
    extent, width = values.shape
    groups = digit_groups(count, radix)
    values = values.reshape((extent,) + tuple(reversed(groups)) + (width // count,))
    stride = 1
    for level, size in enumerate(groups):
        dim = len(groups) - level
        mine = index // stride % size
        total = lax.dynamic_index_in_dim(values, mine, axis=dim, keepdims=False)
        for offset in range(1, size):
            send = lax.dynamic_index_in_dim(values, mine ^ offset, axis=dim, keepdims=False)
            total = total + exchanged(send, axis, offset * stride)
        values = total
        stride *= size
    return values.reshape(extent, width // count)


def all_gather_cols(values, axis, radix=4):
    count = lax.axis_size(axis)
    index = lax.axis_index(axis)
    extent, block = values.shape
    groups = digit_groups(count, radix)
    stride = count
    for size in reversed(groups):
        stride //= size
        mine = index // stride % size
        got = [values] + [exchanged(values, axis, offset * stride) for offset in range(1, size)]
        parts = []
        for slot in range(size):
            part = jnp.zeros_like(values)
            for offset in range(size):
                part = part + jnp.where((slot ^ mine) == offset, got[offset], 0.0)
            parts.append(part)
        values = jnp.stack(parts, values.ndim - 1)
    return values.reshape(extent, block * count)


def scatter_sum_cols(values, axis):
    count = lax.axis_size(axis)
    extent, width = values.shape
    share = width // count
    split = values.reshape(extent, count, share).transpose(1, 0, 2)
    split = split.reshape(count, extent * share // 128, 128)
    joined = lax.all_to_all(split, axis, 0, 0, tiled=True)
    return jnp.sum(joined, axis=0).reshape(extent, share)


def all_reduce_cols(values, axis, widen, radix=4):
    count = lax.axis_size(axis)
    index = lax.axis_index(axis)
    low = min(radix, count)
    high = count // low
    extent, width = values.shape
    values = values.reshape(extent, high, low, width // count)
    mine = index % low
    total = lax.dynamic_index_in_dim(values, mine, axis=2, keepdims=False)
    for offset in range(1, low):
        send = lax.dynamic_index_in_dim(values, mine ^ offset, axis=2, keepdims=False)
        total = total + exchanged(send, axis, offset)
    upper = index // low
    got = [total] + [exchanged(total, axis, offset * low) for offset in range(1, high)]
    summed = jnp.zeros_like(total)
    for slot in range(high):
        term = jnp.zeros_like(total)
        for offset in range(high):
            term = term + jnp.where((slot ^ upper) == offset, got[offset], 0.0)
        summed = summed + term
    summed = widen(summed)
    got = [summed] + [exchanged(summed, axis, offset) for offset in range(1, low)]
    parts = []
    for slot in range(low):
        part = jnp.zeros_like(summed)
        for offset in range(low):
            part = part + jnp.where((slot ^ mine) == offset, got[offset], 0.0)
        parts.append(part)
    return jnp.stack(parts, 2).reshape(summed.shape[0], width)


def resist_section(intensity_term, kernel_taps, target, kern_count, kern_index):
    reach = (kernel_taps.shape[0] - 1) // 2
    flipped = kernel_taps[::-1]
    extent, full_width = intensity_term.shape
    share_cols = full_width // kern_count
    wide = extent + 2 * reach
    bands = lax.optimization_barrier(
        (blur_bands(kernel_taps, wide, 128, 64), blur_bands(flipped, extent, 128, 64))
    )
    goal_cells = padded_2(target, (("slab", 0),), reach).astype(jnp.float32)
    summed = all_reduce_cols(
        intensity_term, "kern", lambda block: padded_2(block, (("slab", 0),), 2 * reach)
    )
    resist = jax.nn.sigmoid(STEEP * (smooth(summed, bands[0], wide, full_width) - LEVEL))
    first_row = lax.axis_index("slab") * extent - reach
    rows = first_row + jnp.arange(wide)
    inside = (rows >= 0) & (rows < lax.axis_size("slab") * extent)
    slope_grad = 2.0 * (resist - goal_cells) * STEEP * resist * (1.0 - resist)
    slope_grad = jnp.where(inside[:, None], slope_grad, 0.0)
    cotangent = smooth(slope_grad, bands[1], extent, full_width)
    resist = lax.dynamic_slice_in_dim(resist[reach : reach + extent], kern_index * share_cols, share_cols, 1)
    return (cotangent, resist)


def to_columns(stacked):
    pieces, extent, width = stacked.shape
    count = lax.axis_size("slab")
    share = width // count
    split = stacked.reshape(pieces, extent, count, share).transpose(2, 0, 1, 3)
    split = split.reshape(count, pieces * extent * share // 128, 128)
    joined = lax.all_to_all(split, "slab", 0, 0, tiled=True)
    return joined.reshape(count, pieces, extent, share).transpose(1, 0, 2, 3)


def to_rows(stacked):
    pieces, count, extent, share = stacked.shape
    split = stacked.transpose(1, 0, 2, 3).reshape(count, pieces * extent * share // 128, 128)
    joined = lax.all_to_all(split, "slab", 0, 0, tiled=True).reshape(count, pieces, extent, share)
    return joined.transpose(1, 2, 0, 3).reshape(pieces, extent, count * share)


def row_tables(count, extent, sign_val):
    num_bits = count.bit_length() - 1
    slab_idx = np.arange(count)
    local_idx = np.arange(extent)
    flipped = reversed_bits(slab_idx, num_bits)
    across = rotation(flipped[:, None] * slab_idx[None, :], count, sign_val)
    twiddle = rotation(flipped[:, None] * local_idx[None, :], count * extent, sign_val)
    within = rotation(local_idx[:, None] * local_idx[None, :], extent, sign_val)
    return (across, twiddle, within)


def rows_forward_t(values):
    count, extent, _ = values[0].shape
    across, twiddle, within = row_tables(count, extent, -1.0)
    values = table_product("ed,dpv->epv", across, values)
    values = complex_mul(values, (twiddle[0][:, :, None], twiddle[1][:, :, None]))
    return table_product("qp,epv->eqv", within, values)


def rows_inverse_t(values):
    count, extent, _ = values[0].shape
    across, twiddle, within = row_tables(count, extent, 1.0)
    values = table_product("pq,eqv->epv", within, values)
    values = complex_mul(values, (twiddle[0][:, :, None], twiddle[1][:, :, None]))
    return table_product("ed,epv->dpv", across, values)


def on_device(mask_level, kernel_spectra, socs_weight, kernel_slot, blur_taps, target):
    extent, full_width = mask_level.shape
    slab_count = lax.axis_size("slab")
    kern_count = lax.axis_size("kern")
    num_bits = slab_count.bit_length() - 1
    inner_len = CQ
    outer_len = full_width // inner_len
    freq_offset = reversed_bits(lax.axis_index("slab"), num_bits)
    kern_index = lax.axis_index("kern")
    kernel_id = jnp.sum(jnp.where(jnp.arange(kernel_slot.shape[0]) == kern_index, kernel_slot, 0))
    weight = jnp.sum(jnp.where(jnp.arange(socs_weight.shape[0]) == kernel_id, socs_weight, 0.0))
    arranged = kernel_spectra[0].reshape(2, extent, inner_len, outer_len).transpose(0, 1, 3, 2)
    arranged = to_columns(arranged.reshape(2, extent, full_width))
    transfer = (arranged[0], arranged[1])
    norm_scale = 1.0 / (full_width * full_width)

    def spectrum(values):
        columns = columns_forward(values, outer_len, inner_len)
        stacked = to_columns(jnp.stack(columns).reshape(2, extent, full_width))
        return rows_forward_t((stacked[0], stacked[1]))

    def back_to_cells(spectral, real_only):
        stacked = to_rows(jnp.stack(rows_inverse_t(spectral)))
        shaped = (
            stacked[0].reshape(extent, outer_len, inner_len),
            stacked[1].reshape(extent, outer_len, inner_len),
        )
        return columns_inverse(shaped, outer_len, inner_len, real_only, norm_scale)

    mask_spec = spectrum((mask_level, None))
    field_val = back_to_cells(complex_mul(transfer, mask_spec), False)
    intensity_term = weight * (field_val[0] * field_val[0] + field_val[1] * field_val[1])
    cotangent, resist = resist_section(intensity_term, blur_taps, target, kern_count, kern_index)
    factor = 2.0 * weight * cotangent
    carried_spec = spectrum((factor * field_val[0], factor * field_val[1]))
    gradient_term = (
        back_to_cells(complex_mul((transfer[0], -transfer[1]), carried_spec), True)
    )
    gradient = scatter_sum_cols(gradient_term, "kern")
    return (gradient, resist)


def solution(mesh):
    placed = (P("slab", None), P("kern", None, "slab", None), P(), P(), P(), P("slab", None))
    return jax.shard_map(
        on_device,
        mesh=mesh,
        in_specs=placed,
        out_specs=(P("slab", "kern"), P("slab", "kern")),
        check_vma=False,
    )
```
